32 devices in a mesh: dom: 8 (over y, x, core), sub: 4 (over z).
Axes of the slice: x: 2, y: 2, z: 4, core: 2. Of those that a mesh axis runs over, the one named last changes fastest.
Arguments:
- positions: bfloat16 [3, 4096], P(None, ('dom', 'sub')), may hold values from 0 to 1
- species: int32 [4096], P(('dom', 'sub')), may hold values from 0 to 1
- neighbours: int32 [64, 4096], P(None, ('dom', 'sub')), may hold values from -1 to 255, as said below
- ghost_rows: int32 [4, 1024], P(None, ('dom', 'sub')), may hold values from 0 to 127
- wavevectors: int32 [3, 12288], replicated, may hold values from -19 to 20, as said below
- embedding: bfloat16 [2, 128], replicated, may hold values from -6 to 6
- w_in: bfloat16 [2, 128, 128], replicated, may hold values from -0.5 to 0.5
- radial: bfloat16 [2, 8, 128], replicated, may hold values from -2 to 2
- norm_gain: bfloat16 [2, 128], replicated, may hold values from 0.25 to 1.75
- w_out: bfloat16 [2, 128, 128], replicated, may hold values from -0.5 to 0.5
- w_charge: bfloat16 [128, 8], replicated, may hold values from -0.5 to 0.5
Outputs:
- potentials: float32 [8, 4096], P(None, ('dom', 'sub'))
- forces: float32 [3, 4096], P(None, ('dom', 'sub'))
The draws below stay inside these ranges and needn't reach their ends.
Inputs may be any that keep to these rules, and one draw needn't show every extreme that they name: `neighbours`: used slots come first in each atom's list, -1 fills the rest, and every list uses 64 // 2 slots or more; an entry below 128 is one of the device's own atoms, else it is ghost number (entry - 128) % 32 of block (entry - 128) // 32 of the table. `wavevectors`: the columns are distinct; the first nonzero component of each column is positive; the sum of the squares of a column is at most 400.
All inputs are finite; a program needn't handle non-finite values.
Results may differ from the reference program's by a relative error of at most 0.0067.
Values may be sent and summed in bfloat16 or wider, within the bound.
No kernel may reach another device: no remote copies, remote signals or barrier semaphores. Data moves between devices by JAX's collectives and lax.ppermute only.
A program may use at most 64 MiB of HBM per device.

```python
import math
import jax
import jax.numpy as jnp
from jax import lax

C = 128
B = 8
Q = 8
K = 12288
NB = 64
LAYERS = 2
REACH = 20
A = 128
G = 32
ATOMS = 4096
N_DOM = 8
N_SUB = 4
DEVICES = 32


def draw_neighbours(key, part):
    key_kind, key_local, key_ghost, key_count = jax.random.split(jax.random.fold_in(key, 11), 4)
    kind = jax.random.randint(key_kind, (NB, ATOMS), 0, 8)
    local = jax.random.randint(key_local, (NB, ATOMS), 0, A)
    ghost = jax.random.randint(key_ghost, (NB, ATOMS), 0, G)
    count = jax.random.randint(key_count, (1, ATOMS), NB // 2, NB + 1)
    entry = jnp.where(kind < 4, local, A + (kind - 4) * G + ghost)
    slot_number = jnp.arange(NB, dtype=jnp.int32)[:, None]
    return jnp.where(slot_number < count, entry, -1).astype(jnp.int32)


def draw_wavevectors(key, part):
    side_len = 2 * REACH + 1
    shuffled = jax.random.permutation(jax.random.fold_in(key, 23), side_len * side_len * side_len).astype(jnp.int32)
    first_comp = shuffled // (side_len * side_len) - REACH
    second_comp = shuffled // side_len % side_len - REACH
    third_comp = shuffled % side_len - REACH
    squared = first_comp * first_comp + second_comp * second_comp + third_comp * third_comp
    upper_half = (first_comp > 0) | (first_comp == 0) & (second_comp > 0) | (first_comp == 0) & (second_comp == 0) & (third_comp > 0)
    inside = upper_half & (squared <= REACH * REACH)
    top_end = (first_comp == REACH) & (second_comp == 0) & (third_comp == 0)
    low_end = (first_comp == 1) & (second_comp == 1 - REACH) & (third_comp == 0)
    order_key = jnp.where(top_end | low_end, 0, jnp.where(inside, 1, 2)).astype(jnp.int32)
    chosen_rows = jnp.argsort(order_key, stable=True)[:K]
    return jnp.stack([first_comp[chosen_rows], second_comp[chosen_rows], third_comp[chosen_rows]]).astype(jnp.int32)


def touch_ends(values, stream_key, smallest, top_value):
    place = [jax.random.randint(jax.random.fold_in(stream_key, axis), (), 0, length) for axis, length in enumerate(values.shape)]
    longest = values.shape.index(max(values.shape))
    next_to = place[:longest] + [(place[longest] + 1) % values.shape[longest]] + place[longest + 1:]
    return values.at[tuple(place)].set(smallest).at[tuple(next_to)].set(top_value)


def steps_of(key, extent, shards, low, largest):
    loudness, own = 1.0, jax.random.fold_in(key, 6)
    for position, blocks in shards:
        draws = jnp.exp(jax.random.uniform(jax.random.fold_in(own, position), (blocks,), jnp.float32, low / len(shards), largest / len(shards)))
        loudness = loudness * jnp.repeat(draws, extent[position] // blocks).reshape([-1 if axis == position else 1 for axis in range(len(extent))])
    return loudness


def centred(key, shape, scale, most, held_as=jnp.bfloat16):
    return jnp.clip(scale * jax.random.normal(key, shape, jnp.float32), -most, most).astype(held_as)


def setup_inputs(seed: int = 0) -> dict:
    keys = jax.random.split(jax.random.key(seed), 12)
    positions = jnp.clip(1.0 * jax.random.uniform(keys[0], (3, ATOMS), jnp.float32) ** steps_of(keys[0], (3, ATOMS), ((1, 32),), -0.2, 0.2), 0.0, 1.0).astype(jnp.bfloat16)
    species = touch_ends(jax.random.randint(keys[1], (ATOMS,), 0, 2), jax.random.fold_in(keys[1], 1), 0, 1).astype(jnp.int32)
    neighbours = draw_neighbours(jax.random.fold_in(keys[11], 71), 0)
    ghost_rows = touch_ends(jax.random.randint(keys[3], (4, G * DEVICES), 0, A), jax.random.fold_in(keys[3], 1), 0, A - 1).astype(jnp.int32)
    wavevectors = draw_wavevectors(jax.random.fold_in(keys[11], 71), 0)
    embedding = centred(keys[5], (2, C), 1.0, 6.0)
    w_in = centred(keys[6], (LAYERS, C, C), C ** -0.5, 0.5)
    radial = centred(keys[7], (LAYERS, B, C), B ** -0.5, 2.0)
    norm_gain = jnp.clip(1.0 + 0.15 * jax.random.normal(keys[8], (LAYERS, C), jnp.float32), 0.25, 1.75).astype(jnp.bfloat16)
    w_out = centred(keys[9], (LAYERS, C, C), C ** -0.5, 0.5)
    w_charge = centred(keys[10], (C, Q), C ** -0.5, 0.5)
    return dict(positions=positions, species=species, neighbours=neighbours, ghost_rows=ghost_rows, wavevectors=wavevectors, embedding=embedding, w_in=w_in, radial=radial, norm_gain=norm_gain, w_out=w_out, w_charge=w_charge)


smearing = 0.005
epsilon = 1e-05
highest = lax.Precision.HIGHEST

def reference(positions, species, neighbours, ghost_rows, wavevectors, embedding, w_in, radial, norm_gain, w_out, w_charge):
    devices = N_DOM * N_SUB
    table_rows = A + 4 * G
    ghost_grid = ghost_rows.reshape(4, N_DOM, N_SUB, G)

    def with_ghosts(local):
        width = local.shape[3]
        picked = []
        for side_number in range(4):
            index_grid = jnp.broadcast_to(ghost_grid[side_number][:, :, :, None], (N_DOM, N_SUB, G, width))
            picked.append(jnp.take_along_axis(local, index_grid, axis=2))
        joined = jnp.concatenate([local, jnp.roll(picked[1], 1, axis=0), jnp.roll(picked[0], -1, axis=0), jnp.roll(picked[3], 1, axis=1), jnp.roll(picked[2], -1, axis=1)], axis=2)
        return joined.reshape(devices, table_rows, width)
    local_coords = positions.reshape(3, N_DOM, N_SUB, A).transpose(1, 2, 3, 0)
    coord_table = with_ghosts(local_coords).astype(jnp.float32)
    lists = neighbours.reshape(NB, devices, A).transpose(1, 0, 2)
    clamped = jnp.maximum(lists, 0)
    live_mask = lists >= 0
    own_coords = positions.astype(jnp.float32).reshape(3, devices, A).transpose(1, 2, 0)
    nearby = jax.vmap(lambda table, chosen: table[chosen])(coord_table, clamped)
    displace = nearby - own_coords[:, None, :, :]
    chord_sq = lax.optimization_barrier(jnp.sum(jnp.sin(math.pi * displace) ** 2, axis=3))
    decay_rates = jnp.exp2(jnp.arange(B, dtype=jnp.float32) - 3.0)
    radial_basis = jnp.exp(-decay_rates[None, :, None, None] * chord_sq[:, None, :, :])
    hidden = jnp.where((species == 1)[:, None], embedding[1][None, :], embedding[0][None, :])
    for layer_number in range(LAYERS):
        projected = jnp.dot(hidden.astype(jnp.float32), w_in[layer_number].astype(jnp.float32), precision=highest, preferred_element_type=jnp.float32).astype(jnp.bfloat16)
        feat_tables = with_ghosts(projected.reshape(N_DOM, N_SUB, A, C))
        radial_layer = radial[layer_number].astype(jnp.float32)

        def one_device(inputs):
            basis_here, clamped_here, live_here, table_here = inputs
            edge_weight = jnp.einsum('bna,bc->nac', basis_here, radial_layer, precision=highest)
            gathered = table_here[clamped_here].astype(jnp.float32)
            return lax.optimization_barrier(jnp.sum(jnp.where(live_here[:, :, None], edge_weight * gathered, 0.0), axis=0))
        message = lax.map(one_device, (radial_basis, clamped, live_mask, feat_tables)).reshape(ATOMS, C)
        normed = message * lax.rsqrt(lax.optimization_barrier(jnp.mean(message * message, axis=1, keepdims=True)) + epsilon)
        normed = normed * norm_gain[layer_number].astype(jnp.float32)[None, :]
        activated = jax.nn.silu(normed).astype(jnp.bfloat16)
        update = jnp.dot(activated.astype(jnp.float32), w_out[layer_number].astype(jnp.float32), precision=highest, preferred_element_type=jnp.float32)
        hidden = (hidden.astype(jnp.float32) + update).astype(jnp.bfloat16)
    charges = jnp.dot(hidden.astype(jnp.float32), w_charge.astype(jnp.float32), precision=highest, preferred_element_type=jnp.float32).T
    wave_float = wavevectors.astype(jnp.float32)
    squared = lax.optimization_barrier(jnp.sum(wave_float * wave_float, axis=0))
    kweight = jnp.exp(-smearing * squared) / squared
    coords = positions.astype(jnp.float32)
    block_len = math.gcd(K, 128)
    block_count = K // block_len
    wave_blocks = wave_float.reshape(3, block_count, block_len).transpose(1, 0, 2)

    def phases(chosen):
        angle = 2.0 * math.pi * jnp.einsum('dk,da->ka', chosen, coords, precision=highest)
        return (jnp.cos(angle), jnp.sin(angle))

    def structure_block(chosen):
        cosines, sines = phases(chosen)
        return jnp.concatenate([jnp.einsum('qa,ka->qk', charges, cosines, precision=highest), jnp.einsum('qa,ka->qk', charges, sines, precision=highest)], axis=0)
    structure = lax.map(structure_block, wave_blocks)
    weighted = structure * kweight.reshape(block_count, 1, block_len)

    def apply_block(carry, inputs):
        potential, force_sum = carry
        chosen, weight_block = inputs
        cosines, sines = phases(chosen)
        cos_weight = weight_block[:Q]
        sin_weight = weight_block[Q:]
        potential = potential + jnp.einsum('qk,ka->qa', cos_weight, cosines, precision=highest)
        potential = potential + jnp.einsum('qk,ka->qa', sin_weight, sines, precision=highest)
        cos_dir = chosen[:, None, :] * cos_weight[None, :, :]
        sin_dir = chosen[:, None, :] * sin_weight[None, :, :]
        inner = jnp.einsum('dqk,ka->dqa', cos_dir, sines, precision=highest)
        inner = inner - jnp.einsum('dqk,ka->dqa', sin_dir, cosines, precision=highest)
        force_sum = force_sum + lax.optimization_barrier(jnp.sum(charges[None, :, :] * inner, axis=1))
        return ((potential, force_sum), None)
    start = (jnp.zeros((Q, ATOMS), jnp.float32), jnp.zeros((3, ATOMS), jnp.float32))
    (potential, force_sum), _ = lax.scan(apply_block, start, (wave_blocks, weighted))
    scale = 1.0 / math.sqrt(ATOMS)
    return (potential * scale, force_sum * scale)
```

```python
import functools
import math

import jax
import jax.numpy as jnp
from jax import lax
from jax.experimental import pallas as pl
from jax.experimental.pallas import tpu as pltpu
from jax.sharding import PartitionSpec as P

f32, bf16, i32 = jnp.float32, jnp.bfloat16, jnp.int32
smearing = 0.005
epsilon = 1e-05
highest = lax.Precision.HIGHEST

reach = 20
harmonics = reach + 1
signed = 2 * reach
pair_groups = 48
pairs = 8 * pair_groups
lane_blocks = pairs // 128
mask_rows = lane_blocks * 2 * signed
common = 8

sin_terms = (3.14159258, -5.16770688, 2.55003138, -0.59804517, 0.07722013)
cos_terms = (0.99999995, -4.93479286, 4.05841191, -1.33188016, 0.21969679)
sends = ((1, 0), (-1, 0), (0, 1), (0, -1))
ghost_order = (1, 0, 3, 2)


def poly(terms, square):
    total = jnp.full_like(square, terms[-1])
    for term in terms[-2::-1]:
        total = total * square + term
    return total


def sin_pi(turns):
    rest = turns - jnp.round(turns)
    return rest * poly(sin_terms, rest * rest)


def cos_sin(turns):
    rest = turns - jnp.round(turns)
    square = rest * rest
    half_sin = rest * poly(sin_terms, square)
    half_cos = poly(cos_terms, square)
    return 1.0 - 2.0 * half_sin * half_sin, 2.0 * half_sin * half_cos


def iota(shape, axis):
    return lax.broadcasted_iota(i32, shape, axis)


def lanes_of(shape, width):
    return lax.div(iota(shape, len(shape) - 1), jnp.int32(width))


def by_block(parts, width):
    which = lanes_of(parts[0].shape, width)
    out = parts[-1]
    for number in range(len(parts) - 2, -1, -1):
        out = jnp.where(which == number, parts[number], out)
    return out


def row_of(values, row, count):
    return jnp.broadcast_to(values[row : row + 1], (count,) + values.shape[1:])


def take_lanes(row_values, index):
    return jnp.take_along_axis(row_values, index, axis=1)


def dot(left, right, dims, precision=None):
    return lax.dot_general(left, right, ((dims[0], dims[1]), ((), ())), precision=precision, preferred_element_type=f32)


def pack_kernel(sizes, pos_ref, spec_ref, nbr_ref, rows_ref, out_ref):
    n_dom, n_sub = sizes
    count, _, atoms = out_ref.shape
    ghosts = rows_ref.shape[1]
    slots = nbr_ref.shape[0]
    quarter = slots // 4
    order = jnp.concatenate([rows_ref[row : row + 1, :] for row in ghost_order], axis=1)
    head = jnp.concatenate(
        [
            pos_ref[...].astype(f32),
            spec_ref[...].astype(f32),
            order.astype(f32),
            jnp.zeros((common - 5, atoms), f32),
        ],
        axis=0,
    )
    whole = jnp.concatenate([head, jnp.zeros((quarter, atoms), f32)], axis=0).astype(bf16)
    for device in range(count):
        out_ref[device] = whole
    index = jnp.broadcast_to(order, (8, atoms))
    lists = [take_lanes(nbr_ref[8 * s : 8 * s + 8, :], index).astype(f32) for s in range(slots // 8)]
    per = quarter // 8
    dom, sub = lax.axis_index("dom"), lax.axis_index("sub")
    for block, (dom_step, sub_step) in enumerate(sends):
        rows = []
        for piece in range(per):
            parts = [
                pltpu.roll(lists[r * per + piece], (ghosts * (r - block)) % atoms, 1) if r != block else lists[r * per + piece]
                for r in range(4)
            ]
            rows.append(by_block(parts, ghosts))
        target = lax.rem(dom + dom_step + n_dom, n_dom) * n_sub + lax.rem(sub + sub_step + n_sub, n_sub)
        out_ref[target, common:, :] = jnp.concatenate(rows, axis=0).astype(bf16)


def first_layer_sums(lists, tables, centre, ghosts, bases):
    total = [[None] * bases for _ in range(2)]
    for listed in lists:
        index = jnp.maximum(listed, 0)
        low = jnp.bitwise_and(index, 127)
        is_ghost = index >= 128
        found = []
        for quantity in range(4):
            parts = [
                jnp.where(is_ghost, take_lanes(row_of(outer, quantity, 8), low), take_lanes(row_of(inner, quantity, 8), low))
                for inner, outer in tables
            ]
            found.append(by_block(parts, ghosts) if len(parts) > 1 else parts[0])
        chord = jnp.zeros(low.shape, f32)
        for axis in range(3):
            wave = sin_pi(found[axis] - row_of(centre, axis, 8))
            chord = chord + wave * wave
        first = jnp.where(listed >= 0, jnp.exp(-0.125 * chord), 0.0)
        for kind in range(2):
            power = jnp.where((found[3] > 0.5) if kind else (found[3] <= 0.5), first, 0.0)
            for basis in range(bases):
                if basis:
                    power = power * power
                total[kind][basis] = power if total[kind][basis] is None else total[kind][basis] + power
    return jnp.concatenate(total[0] + total[1], axis=0)


def wave_mask(wave_ref, rows, device):
    first = wave_ref[0:1, :]
    second = wave_ref[1:2, :]
    third = wave_ref[2:3, :]
    size = jnp.abs(second)
    pair = jnp.where(
        size < 8,
        8 * first + size,
        jnp.where(size < 16, 160 + 8 * first + size, jnp.where(size < 20, 304 + 4 * first + size, 376)),
    )
    side = jnp.where(second < 0, 1, 0)
    block = jnp.right_shift(pair, 7)
    lane = jnp.bitwise_and(pair, 127)
    row = (block * 2 + side) * signed + third + (reach - 1) - device * rows
    inside = (row >= 0) & (row < rows)
    key = jnp.where(inside, jnp.right_shift(lane, 5) * rows + row, -1)
    low = jnp.bitwise_and(lane, 31)
    total_k = key.shape[1]
    left = jnp.where(iota((4 * rows, total_k), 0) == key, 1.0, 0.0).astype(bf16)
    right = jnp.where(iota((32, total_k), 0) == low, 1.0, 0.0).astype(bf16)
    found = dot(left, right, ((1,), (1,)))
    spread = jnp.concatenate([found] * 4, axis=1)
    return by_block([spread[q * rows : (q + 1) * rows] for q in range(4)], 32)


def normed_silu(message, gain):
    normed = message * lax.rsqrt(jnp.mean(message * message, axis=0, keepdims=True) + epsilon) * gain
    return (normed / (1.0 + jnp.exp(-normed))).astype(bf16)


def charge_kernel(
    sizes,
    cells,
    recv_ref,
    nbr_ref,
    wave_ref,
    emb_ref,
    w_in_ref,
    radial_ref,
    gain_ref,
    w_out_ref,
    w_charge_ref,
    out_ref,
    charge_ref,
):
    n_dom, n_sub = sizes
    count = out_ref.shape[0]
    atoms = nbr_ref.shape[1]
    slots = nbr_ref.shape[0]
    bases = radial_ref.shape[1]
    channels = w_in_ref.shape[1]
    ghosts = atoms // 4
    quarter = slots // 4
    dom, sub = lax.axis_index("dom"), lax.axis_index("sub")

    def device_at(dom_step, sub_step):
        return lax.rem(dom + dom_step + 2 * n_dom, n_dom) * n_sub + lax.rem(sub + sub_step + 2 * n_sub, n_sub)

    origins = tuple((-dom_step, -sub_step) for dom_step, sub_step in sends)
    data, picked = {}, {}
    for base in ((0, 0),) + origins:
        for step in ((0, 0),) + origins:
            key = (base[0] + step[0], base[1] + step[1])
            if key not in data:
                data[key] = recv_ref[device_at(*key), 0:common, :].astype(f32)
                index = row_of(data[key], 4, common).astype(i32)
                picked[key] = take_lanes(data[key], index)

    def table(key):
        return data[key], by_block([picked[(key[0] + s[0], key[1] + s[1])] for s in origins], ghosts)

    own = data[(0, 0)]
    own_table = table((0, 0))
    own_ghosts = own_table[1]

    own_lists = [nbr_ref[8 * s : 8 * s + 8, :] for s in range(slots // 8)]
    sent = [recv_ref[device_at(*key), common:, :].astype(f32) for key in origins]
    ghost_lists = []
    for r in range(4):
        for piece in range(quarter // 8):
            parts = []
            for block in range(4):
                part = sent[block][8 * piece : 8 * piece + 8]
                shift = (ghosts * (block - r)) % atoms
                parts.append(pltpu.roll(part, shift, 1) if shift else part)
            ghost_lists.append(by_block(parts, ghosts).astype(i32))

    sums = jnp.concatenate(
        [
            first_layer_sums(own_lists, [own_table], own, ghosts, bases),
            first_layer_sums(ghost_lists, [table(key) for key in origins], own_ghosts, ghosts, bases),
        ],
        axis=1,
    )
    kinds = jnp.concatenate([emb_ref[...].astype(f32), jnp.zeros((6, channels), f32)], axis=0).astype(bf16)
    two_feats = dot(kinds, w_in_ref[0], ((1,), (0,))).astype(bf16).astype(f32)
    radial_first = radial_ref[0].astype(f32)
    weights = jnp.concatenate(
        [
            jnp.broadcast_to(radial_first[basis : basis + 1] * two_feats[kind : kind + 1], (8, channels))
            for kind in range(2)
            for basis in range(bases)
        ],
        axis=0,
    )
    message = dot(weights, sums, ((0,), (0,)), highest)

    params = jnp.concatenate(
        [radial_ref[1].astype(f32), gain_ref[...].astype(f32), jnp.zeros((16 - bases - 2, channels), f32)], axis=0
    ).astype(bf16)
    spread = jnp.where(iota((16, 16 * atoms), 0) == lanes_of((16, 16 * atoms), atoms), 1.0, 0.0).astype(bf16)
    columns = dot(params, spread, ((0,), (0,)))

    def column(number):
        return columns[:, number * atoms : (number + 1) * atoms]

    gain_first = column(bases)
    activated = normed_silu(message, jnp.concatenate([gain_first, gain_first], axis=1))
    species = jnp.concatenate([own[3:4], own_ghosts[3:4]], axis=1)
    kind_rows = iota((8, 2 * atoms), 0)
    choice = jnp.where((kind_rows < 2) & (jnp.where(species > 0.5, 1, 0) == kind_rows), 1.0, 0.0).astype(bf16)
    hidden = dot(kinds, choice, ((0,), (0,)))
    hidden = (hidden + dot(w_out_ref[0], activated, ((0,), (0,)))).astype(bf16)
    feats = dot(w_in_ref[1], hidden, ((0,), (0,))).astype(bf16)

    near = [cos_sin(jnp.concatenate([own, own_ghosts], axis=1))]
    is_axis = iota((8, 2 * atoms), 0) < 3
    cosines = jnp.where(is_axis, near[0][0], 0.0)
    sines = jnp.where(is_axis, near[0][1], 0.0)
    waves = jnp.concatenate([cosines, sines], axis=0)
    chord = 1.5 - 0.5 * dot(waves, waves[:, :atoms], ((0,), (0,)), highest)
    listed = [nbr_ref[8 * s : 8 * s + 8, :].astype(f32) for s in range(slots // 8)]
    halves = []
    for half in range(2):
        row_number = (iota((atoms, atoms), 0) + half * atoms).astype(f32)
        times = jnp.zeros((atoms, atoms), f32)
        for slot in range(slots):
            times = times + jnp.where(row_number == row_of(listed[slot // 8], slot % 8, atoms), 1.0, 0.0)
        halves.append(times)
    times = jnp.concatenate(halves, axis=0)
    power = jnp.exp(-0.125 * chord)
    message = jnp.zeros((channels, atoms), f32)
    for basis in range(bases):
        if basis:
            power = power * power
        weighted = times * power
        high = weighted.astype(bf16)
        low = (weighted - high.astype(f32)).astype(bf16)
        mixed = dot(feats, high, ((1,), (0,))) + dot(feats, low, ((1,), (0,)))
        message = message + column(basis) * mixed
    activated = normed_silu(message, column(bases + 1))
    hidden = (hidden[:, :atoms].astype(f32) + dot(w_out_ref[1], activated, ((0,), (0,)))).astype(bf16)
    charges = dot(w_charge_ref[...], hidden, ((0,), (0,)))
    charge_ref[...] = charges
    mask = wave_mask(wave_ref, cells, dom * n_sub + sub)
    fill = out_ref.shape[1] - charges.shape[0] - cells
    pieces = [charges, mask] + ([jnp.zeros((fill, atoms), f32)] if fill else [])
    block = jnp.concatenate(pieces, axis=0).astype(bf16)
    for device in range(count):
        out_ref[device] = block


def harmonic_tables(coords):
    lanes = coords.shape[1]
    step = iota((8, lanes), 0)
    big = jnp.where(step < 3, 8.0, 16.0)
    far = jnp.concatenate([coords[0:3], coords[0:3], coords[0:2]], axis=0)
    jump_cos, jump_sin = cos_sin(big * far)
    tables = []
    for axis in range(3):
        cos_low, sin_low = cos_sin(step.astype(f32) * row_of(coords, axis, 8))
        cosines, sines = [cos_low], [sin_low]
        for jump in (axis, 3 + axis):
            c, s = row_of(jump_cos, jump, 8), row_of(jump_sin, jump, 8)
            cosines.append(cos_low * c - sin_low * s)
            sines.append(sin_low * c + cos_low * s)
        tables.append((cosines, sines))
    return tables


def pair_rows(first, second):
    lanes = first[0].shape[1]
    lower = iota((8, lanes), 0) < 4

    def of(number):
        return row_of(first[number // 8], number % 8, 8)

    groups = [of(h) * second[0] for h in range(21)]
    groups += [of(h) * second[1] for h in range(19)]
    swapped = pltpu.roll(second[2], 4, 0)
    tail = jnp.where(lower, second[2], swapped)
    groups += [jnp.where(lower, of(2 * g), of(2 * g + 1)) * tail for g in range(7)]
    groups.append(of(0) * swapped)
    return groups


def pair_values(numbers):
    tail = numbers - 320
    first = jnp.where(
        numbers < 168,
        jnp.right_shift(numbers, 3),
        jnp.where(numbers < 320, jnp.right_shift(numbers - 168, 3), jnp.where(numbers < 376, jnp.right_shift(tail, 2), 0)),
    )
    second = jnp.where(
        numbers < 168,
        jnp.bitwise_and(numbers, 7),
        jnp.where(
            numbers < 320, jnp.bitwise_and(numbers, 7) + 8, jnp.where(numbers < 376, jnp.bitwise_and(tail, 3) + 16, 20)
        ),
    )
    return first, second


def ewald_kernel(sizes, cells, total_atoms, recv_ref, sum_ref, charge_ref, pos_ref, pot_ref, force_ref, grid_ref, left_ref, prod_ref, mask_ref, mix_ref):
    n_dom, n_sub = sizes
    latent, atoms = charge_ref.shape
    count = recv_ref.shape[0]
    chunk = grid_ref.shape[1] // atoms
    rows = latent * 2 * harmonics

    def build(device, place):
        coords = recv_ref[device, 0:common, :].astype(f32)
        tables = harmonic_tables(coords)
        spot = pl.ds(pl.multiple_of(place * atoms, atoms), atoms)
        charge = sum_ref[device, 0:latent, :].astype(f32)
        left = []
        for kind in range(2):
            left += [charge * row_of(tables[2][kind][m // 8], m % 8, latent) for m in range(harmonics)]
        for at in range(0, 2 * harmonics, 2):
            left_ref[at * latent : (at + 2) * latent, spot] = jnp.concatenate(left[at : at + 2], axis=0).astype(bf16)
        for kind in range(4):
            groups = pair_rows(tables[0][kind // 2], tables[1][kind % 2])
            for at in range(0, pair_groups, 2):
                start = kind * pairs + at * 8
                grid_ref[start : start + 16, spot] = jnp.concatenate(groups[at : at + 2], axis=0).astype(bf16)

    def whole_chunk(number, carry):
        def one(place, inner):
            build(number * chunk + place, place)
            return inner

        lax.fori_loop(0, chunk, one, 0)

        def tile(column, inner):
            spot = pl.ds(pl.multiple_of(column * 256, 256), 256)
            part = dot(left_ref[...], grid_ref[spot, :], ((1,), (1,)))

            @pl.when(number == 0)
            def _():
                prod_ref[:, spot] = part

            @pl.when(number > 0)
            def _():
                prod_ref[:, spot] = prod_ref[:, spot] + part

            return inner

        return lax.fori_loop(0, 4 * pairs // 256, tile, carry)

    lax.fori_loop(0, count // chunk, whole_chunk, 0)

    for device in range(-(-mask_rows // cells)):
        mask_ref[device * cells : (device + 1) * cells, :] = sum_ref[device, latent : latent + cells, :].astype(f32)
    first, second = pair_values(iota((8, pairs), 1))
    flat = (first * first + second * second).astype(f32)
    for m in range(harmonics):
        square = flat + float(m * m)
        square = jnp.maximum(square, 1.0)
        decay = jnp.exp(-smearing * square) / square
        for block in range(lane_blocks):
            factor = decay[:, block * 128 : (block + 1) * 128]

            def cell(side, third):
                row = (block * 2 + side) * signed + third + reach - 1
                return jnp.broadcast_to(mask_ref[row : row + 1, :], (8, 128)) * factor

            up = [cell(side, m) for side in range(2)]
            if 0 < m < reach:
                down = [cell(side, -m) for side in range(2)]
                upper = [up[side] + down[side] for side in range(2)]
                lower = [up[side] - down[side] for side in range(2)]
            else:
                upper = lower = up
            weight = (upper[0] + upper[1], upper[0] - upper[1], lower[0] + lower[1], lower[0] - lower[1])

            def at(u, v, w):
                row = (u * harmonics + m) * latent
                col = (v * 2 + w) * pairs + block * 128
                return slice(row, row + latent), slice(col, col + 128)

            real = (at(0, 0, 0), at(0, 1, 1), at(1, 1, 0), at(1, 0, 1))
            imag = (at(0, 1, 0), at(0, 0, 1), at(1, 0, 0), at(1, 1, 1))
            for places, signs in ((real, (1, -1, -1, -1)), (imag, (1, 1, 1, -1))):
                values = [prod_ref[place] for place in places]
                for j, place in enumerate(places):
                    mixed = None
                    for i, value in enumerate(values):
                        term = weight[i ^ j] * value
                        if mixed is None:
                            mixed = term if signs[i] == signs[j] else -term
                        else:
                            mixed = mixed + term if signs[i] == signs[j] else mixed - term
                    mix_ref[place] = mixed

    coords = jnp.concatenate([pos_ref[...].astype(f32), jnp.zeros((5, atoms), f32)], axis=0)
    tables = harmonic_tables(coords)
    first, second = pair_values(iota((pairs, atoms), 0))
    first, second = first.astype(f32), second.astype(f32)
    basis = [jnp.concatenate(pair_rows(tables[0][kind // 2], tables[1][kind % 2]), axis=0) for kind in range(4)]
    along_x = [-first * basis[2], -first * basis[3], first * basis[0], first * basis[1]]
    along_y = [-second * basis[1], second * basis[0], -second * basis[3], second * basis[2]]
    right = jnp.concatenate(
        [jnp.concatenate(part, axis=0).astype(bf16) for part in (basis, along_x, along_y)], axis=1
    )
    product = dot(mix_ref[...].astype(bf16), right, ((1,), (0,)))
    potential = jnp.zeros((latent, atoms), f32)
    slopes = [jnp.zeros((latent, atoms), f32) for _ in range(3)]
    for u in range(2):
        for m in range(harmonics):
            factor = row_of(tables[2][u][m // 8], m % 8, latent)
            turned = row_of(tables[2][1 - u][m // 8], m % 8, latent) * float(m if u else -m)
            row = (u * harmonics + m) * latent
            part = [product[row : row + latent, d * atoms : (d + 1) * atoms] for d in range(3)]
            potential = potential + factor * part[0]
            slopes[0] = slopes[0] + factor * part[1]
            slopes[1] = slopes[1] + factor * part[2]
            slopes[2] = slopes[2] + turned * part[0]
    scale = 1.0 / math.sqrt(total_atoms)
    pot_ref[...] = potential * scale
    charge = charge_ref[...]
    for d in range(3):
        force_ref[d : d + 1, :] = jnp.sum(charge * slopes[d], axis=0, keepdims=True) * -scale


def vmem(count):
    return [pl.BlockSpec(memory_space=pltpu.VMEM)] * count


def per_device(
    positions,
    species,
    neighbours,
    ghost_rows,
    wavevectors,
    embedding,
    w_in,
    radial,
    norm_gain,
    w_out,
    w_charge,
):
    axes = ("dom", "sub")
    sizes = (lax.axis_size("dom"), lax.axis_size("sub"))
    count = sizes[0] * sizes[1]
    atoms = positions.shape[1]
    latent = w_charge.shape[1]
    slots = neighbours.shape[0]
    outgoing = pl.pallas_call(
        functools.partial(pack_kernel, sizes),
        out_shape=jax.ShapeDtypeStruct((count, common + slots // 4, atoms), bf16),
        in_specs=vmem(4),
        out_specs=vmem(1)[0],
    )(positions, species[None, :], neighbours, ghost_rows)
    received = lax.all_to_all(outgoing, axes, 0, 0, tiled=True)
    cells = -(-mask_rows // count)
    rows_out = -(-(latent + cells) // 8) * 8
    outgoing, charges = pl.pallas_call(
        functools.partial(charge_kernel, sizes, cells),
        out_shape=(
            jax.ShapeDtypeStruct((count, rows_out, atoms), bf16),
            jax.ShapeDtypeStruct((latent, atoms), f32),
        ),
        in_specs=vmem(9),
        out_specs=tuple(vmem(2)),
    )(received, neighbours, wavevectors, embedding, w_in, radial, norm_gain, w_out, w_charge)
    sums = lax.all_to_all(outgoing, axes, 0, 0, tiled=True)
    chunk = math.gcd(count, 32)
    rows = latent * 2 * harmonics
    return pl.pallas_call(
        functools.partial(ewald_kernel, sizes, cells, atoms * count),
        out_shape=(
            jax.ShapeDtypeStruct((latent, atoms), f32),
            jax.ShapeDtypeStruct((3, atoms), f32),
        ),
        in_specs=vmem(4),
        out_specs=tuple(vmem(2)),
        scratch_shapes=[
            pltpu.VMEM((4 * pairs, chunk * atoms), bf16),
            pltpu.VMEM((rows, chunk * atoms), bf16),
            pltpu.VMEM((rows, 4 * pairs), f32),
            pltpu.VMEM((-(-mask_rows // cells) * cells, 128), f32),
            pltpu.VMEM((rows, 4 * pairs), f32),
        ],
    )(received, sums, charges, positions)


def solution(mesh):
    split = P(None, ("dom", "sub"))
    return jax.shard_map(
        per_device,
        mesh=mesh,
        in_specs=(split, P(("dom", "sub")), split, split) + (P(),) * 7,
        out_specs=(split, split),
        check_vma=False,
    )
```

```python
import functools
import math

import jax
import jax.numpy as jnp
from jax import lax
from jax.experimental import pallas as pl
from jax.experimental.pallas import tpu as pltpu
from jax.sharding import PartitionSpec as P

f32, bf16, i32 = jnp.float32, jnp.bfloat16, jnp.int32
smearing = 0.005
epsilon = 1e-05
highest = lax.Precision.HIGHEST

reach = 20
harmonics = reach + 1
signed = 2 * reach
pair_groups = 48
pairs = 8 * pair_groups
lane_blocks = pairs // 128
mask_rows = lane_blocks * 2 * signed
common = 8

sin_terms = (3.14159258, -5.16770688, 2.55003138, -0.59804517, 0.07722013)
cos_terms = (0.99999995, -4.93479286, 4.05841191, -1.33188016, 0.21969679)
sends = ((1, 0), (-1, 0), (0, 1), (0, -1))
ghost_order = (1, 0, 3, 2)


def poly(terms, square):
    total = jnp.full_like(square, terms[-1])
    for term in terms[-2::-1]:
        total = total * square + term
    return total


def sin_pi(turns):
    rest = turns - jnp.round(turns)
    return rest * poly(sin_terms, rest * rest)


def cos_sin(turns):
    rest = turns - jnp.round(turns)
    square = rest * rest
    half_sin = rest * poly(sin_terms, square)
    half_cos = poly(cos_terms, square)
    return 1.0 - 2.0 * half_sin * half_sin, 2.0 * half_sin * half_cos


def iota(shape, axis):
    return lax.broadcasted_iota(i32, shape, axis)


def lanes_of(shape, width):
    return lax.div(iota(shape, len(shape) - 1), jnp.int32(width))


def by_block(parts, width):
    which = lanes_of(parts[0].shape, width)
    out = parts[-1]
    for number in range(len(parts) - 2, -1, -1):
        out = jnp.where(which == number, parts[number], out)
    return out


def row_of(values, row, count):
    return jnp.broadcast_to(values[row : row + 1], (count,) + values.shape[1:])


def take_lanes(row_values, index):
    return jnp.take_along_axis(row_values, index, axis=1)


def dot(left, right, dims, precision=None):
    return lax.dot_general(left, right, ((dims[0], dims[1]), ((), ())), precision=precision, preferred_element_type=f32)


def pack_kernel(sizes, pos_ref, spec_ref, nbr_ref, rows_ref, out_ref):
    n_dom, n_sub = sizes
    count, _, atoms = out_ref.shape
    ghosts = rows_ref.shape[1]
    slots = nbr_ref.shape[0]
    quarter = slots // 4
    order = jnp.concatenate([rows_ref[row : row + 1, :] for row in ghost_order], axis=1)
    head = jnp.concatenate(
        [
            pos_ref[...].astype(f32),
            spec_ref[...].astype(f32),
            order.astype(f32),
            jnp.zeros((common - 5, atoms), f32),
        ],
        axis=0,
    )
    whole = jnp.concatenate([head, jnp.zeros((quarter, atoms), f32)], axis=0).astype(bf16)
    for device in range(count):
        out_ref[device] = whole
    index = jnp.broadcast_to(order, (8, atoms))
    lists = [take_lanes(nbr_ref[8 * s : 8 * s + 8, :], index).astype(f32) for s in range(slots // 8)]
    per = quarter // 8
    dom, sub = lax.axis_index("dom"), lax.axis_index("sub")
    for block, (dom_step, sub_step) in enumerate(sends):
        rows = []
        for piece in range(per):
            parts = [
                pltpu.roll(lists[r * per + piece], (ghosts * (r - block)) % atoms, 1) if r != block else lists[r * per + piece]
                for r in range(4)
            ]
            rows.append(by_block(parts, ghosts))
        target = lax.rem(dom + dom_step + n_dom, n_dom) * n_sub + lax.rem(sub + sub_step + n_sub, n_sub)
        out_ref[target, common:, :] = jnp.concatenate(rows, axis=0).astype(bf16)


def first_layer_sums(lists, tables, centre, ghosts, bases):
    total = [[None] * bases for _ in range(2)]
    for listed in lists:
        index = jnp.maximum(listed, 0)
        low = jnp.bitwise_and(index, 127)
        is_ghost = index >= 128
        found = []
        for quantity in range(4):
            parts = [
                jnp.where(is_ghost, take_lanes(row_of(outer, quantity, 8), low), take_lanes(row_of(inner, quantity, 8), low))
                for inner, outer in tables
            ]
            found.append(by_block(parts, ghosts) if len(parts) > 1 else parts[0])
        chord = jnp.zeros(low.shape, f32)
        for axis in range(3):
            wave = sin_pi(found[axis] - row_of(centre, axis, 8))
            chord = chord + wave * wave
        first = jnp.where(listed >= 0, jnp.exp(-0.125 * chord), 0.0)
        for kind in range(2):
            power = jnp.where((found[3] > 0.5) if kind else (found[3] <= 0.5), first, 0.0)
            for basis in range(bases):
                if basis:
                    power = power * power
                total[kind][basis] = power if total[kind][basis] is None else total[kind][basis] + power
    return jnp.concatenate(total[0] + total[1], axis=0)


def wave_mask(wave_ref, rows, device):
    first = wave_ref[0:1, :]
    second = wave_ref[1:2, :]
    third = wave_ref[2:3, :]
    size = jnp.abs(second)
    pair = jnp.where(
        size < 8,
        8 * first + size,
        jnp.where(size < 16, 160 + 8 * first + size, jnp.where(size < 20, 304 + 4 * first + size, 376)),
    )
    side = jnp.where(second < 0, 1, 0)
    block = jnp.right_shift(pair, 7)
    lane = jnp.bitwise_and(pair, 127)
    row = (block * 2 + side) * signed + third + (reach - 1) - device * rows
    inside = (row >= 0) & (row < rows)
    key = jnp.where(inside, jnp.right_shift(lane, 5) * rows + row, -1)
    low = jnp.bitwise_and(lane, 31)
    total_k = key.shape[1]
    left = jnp.where(iota((4 * rows, total_k), 0) == key, 1.0, 0.0).astype(bf16)
    right = jnp.where(iota((32, total_k), 0) == low, 1.0, 0.0).astype(bf16)
    found = dot(left, right, ((1,), (1,)))
    spread = jnp.concatenate([found] * 4, axis=1)
    return by_block([spread[q * rows : (q + 1) * rows] for q in range(4)], 32)


def normed_silu(message, gain):
    normed = message * lax.rsqrt(jnp.mean(message * message, axis=0, keepdims=True) + epsilon) * gain
    return (normed / (1.0 + jnp.exp(-normed))).astype(bf16)


def ready_kernel(sizes, cells, nbr_ref, wave_ref, emb_ref, w_in_ref, radial_ref, gain_ref, w_out_ref, w_charge_ref, times_ref, column_ref, weight_ref, turned_ref, mask_ref, list_ref):
    atoms = nbr_ref.shape[1]
    slots = nbr_ref.shape[0]
    bases = radial_ref.shape[1]
    channels = w_in_ref.shape[1]
    latent = w_charge_ref.shape[0]

    kinds = jnp.concatenate([emb_ref[...].astype(f32), jnp.zeros((6, channels), f32)], axis=0).astype(bf16)
    two_feats = dot(kinds, w_in_ref[0], ((1,), (0,))).astype(bf16).astype(f32)
    radial_first = radial_ref[0].astype(f32)
    weights = jnp.concatenate(
        [
            jnp.broadcast_to(radial_first[basis : basis + 1] * two_feats[kind : kind + 1], (8, channels))
            for kind in range(2)
            for basis in range(bases)
        ],
        axis=0,
    )
    weight_ref[...] = weights.T
    params = jnp.concatenate(
        [radial_ref[1].astype(f32), gain_ref[...].astype(f32), jnp.zeros((16 - bases - 2, channels), f32)], axis=0
    ).astype(bf16)
    width = column_ref.shape[1]
    spread = jnp.where(iota((16, width), 0) == lanes_of((16, width), atoms), 1.0, 0.0).astype(bf16)
    column_ref[...] = dot(params, spread, ((0,), (0,)))
    for place, weight in enumerate((w_out_ref[0], w_in_ref[1], w_out_ref[1])):
        turned_ref[place * channels : (place + 1) * channels, :] = weight.astype(f32).T.astype(bf16)
    turned_ref[3 * channels : 3 * channels + 16, :] = jnp.concatenate(
        [w_charge_ref[...].astype(f32), emb_ref[...].astype(f32), jnp.zeros((16 - 2 - latent, channels), f32)], axis=0
    ).astype(bf16)
    listed = [nbr_ref[8 * s : 8 * s + 8, :].astype(f32) for s in range(slots // 8)]
    for half in range(2):
        row_number = (iota((atoms, atoms), 0) + half * atoms).astype(f32)
        times = jnp.zeros((atoms, atoms), f32)
        for slot in range(slots):
            times = times + jnp.where(row_number == row_of(listed[slot // 8], slot % 8, atoms), 1.0, 0.0)
        times_ref[half * atoms : (half + 1) * atoms, :] = times
    device = lax.axis_index("dom") * sizes[1] + lax.axis_index("sub")
    mask_ref[...] = wave_mask(wave_ref, cells, device)
    list_ref[...] = nbr_ref[...]


def charge_kernel(
    sizes,
    cells,
    recv_ref,
    times_ref,
    column_ref,
    weight_ref,
    turned_ref,
    mask_ref,
    nbr_ref,
    out_ref,
    charge_ref,
):
    n_dom, n_sub = sizes
    count = out_ref.shape[0]
    atoms = nbr_ref.shape[1]
    slots = nbr_ref.shape[0]
    channels = column_ref.shape[0]
    bases = column_ref.shape[1] // atoms - 2
    latent = charge_ref.shape[0]
    ghosts = atoms // 4
    quarter = slots // 4
    dom, sub = lax.axis_index("dom"), lax.axis_index("sub")

    def device_at(dom_step, sub_step):
        return lax.rem(dom + dom_step + 2 * n_dom, n_dom) * n_sub + lax.rem(sub + sub_step + 2 * n_sub, n_sub)

    origins = tuple((-dom_step, -sub_step) for dom_step, sub_step in sends)
    data, picked = {}, {}
    for base in ((0, 0),) + origins:
        for step in ((0, 0),) + origins:
            key = (base[0] + step[0], base[1] + step[1])
            if key not in data:
                data[key] = recv_ref[device_at(*key), 0:common, :].astype(f32)
                index = row_of(data[key], 4, common).astype(i32)
                picked[key] = take_lanes(data[key], index)

    def table(key):
        return data[key], by_block([picked[(key[0] + s[0], key[1] + s[1])] for s in origins], ghosts)

    own = data[(0, 0)]
    own_table = table((0, 0))
    own_ghosts = own_table[1]

    own_lists = [nbr_ref[8 * s : 8 * s + 8, :] for s in range(slots // 8)]
    sent = [recv_ref[device_at(*key), common:, :].astype(f32) for key in origins]
    ghost_lists = []
    for r in range(4):
        for piece in range(quarter // 8):
            parts = []
            for block in range(4):
                part = sent[block][8 * piece : 8 * piece + 8]
                shift = (ghosts * (block - r)) % atoms
                parts.append(pltpu.roll(part, shift, 1) if shift else part)
            ghost_lists.append(by_block(parts, ghosts).astype(i32))

    sums = jnp.concatenate(
        [
            first_layer_sums(own_lists, [own_table], own, ghosts, bases),
            first_layer_sums(ghost_lists, [table(key) for key in origins], own_ghosts, ghosts, bases),
        ],
        axis=1,
    )
    message = dot(weight_ref[...], sums, ((1,), (0,)), highest)

    def column(number):
        return column_ref[:, number * atoms : (number + 1) * atoms]

    def turned(place):
        return turned_ref[place * channels : (place + 1) * channels, :]

    gain_first = column(bases)
    activated = normed_silu(message, jnp.concatenate([gain_first, gain_first], axis=1))
    species = jnp.concatenate([own[3:4], own_ghosts[3:4]], axis=1)
    kind_rows = iota((16, 2 * atoms), 0) - latent
    choice = jnp.where(jnp.where(species > 0.5, 1, 0) == kind_rows, 1.0, 0.0).astype(bf16)
    last = turned_ref[3 * channels : 3 * channels + 16, :]
    hidden = dot(last, choice, ((0,), (0,)))
    hidden = (hidden + dot(turned(0), activated, ((1,), (0,)))).astype(bf16)
    feats = dot(turned(1), hidden, ((1,), (0,))).astype(bf16)

    cosines, sines = cos_sin(jnp.concatenate([own, own_ghosts], axis=1))
    is_axis = iota((8, 2 * atoms), 0) < 3
    waves = jnp.concatenate([jnp.where(is_axis, cosines, 0.0), jnp.where(is_axis, sines, 0.0)], axis=0)
    chord = 1.5 - 0.5 * dot(waves, waves[:, :atoms], ((0,), (0,)), highest)
    times = times_ref[...]
    power = jnp.exp(-0.125 * chord)
    message = jnp.zeros((channels, atoms), f32)
    for basis in range(bases):
        if basis:
            power = power * power
        weighted = times * power
        high = weighted.astype(bf16)
        low = (weighted - high.astype(f32)).astype(bf16)
        mixed = dot(feats, high, ((1,), (0,))) + dot(feats, low, ((1,), (0,)))
        message = message + column(basis) * mixed
    activated = normed_silu(message, column(bases + 1))
    hidden = (hidden[:, :atoms].astype(f32) + dot(turned(2), activated, ((1,), (0,)))).astype(bf16)
    charges = dot(last, hidden, ((1,), (0,)))[:latent]
    charge_ref[...] = charges
    fill = out_ref.shape[1] - latent - cells
    pieces = [charges, mask_ref[...]] + ([jnp.zeros((fill, atoms), f32)] if fill else [])
    block = jnp.concatenate(pieces, axis=0).astype(bf16)
    for device in range(count):
        out_ref[device] = block


def harmonic_tables(coords):
    lanes = coords.shape[1]
    step = iota((8, lanes), 0)
    big = jnp.where(step < 3, 8.0, 16.0)
    far = jnp.concatenate([coords[0:3], coords[0:3], coords[0:2]], axis=0)
    jump_cos, jump_sin = cos_sin(big * far)
    tables = []
    for axis in range(3):
        cos_low, sin_low = cos_sin(step.astype(f32) * row_of(coords, axis, 8))
        cosines, sines = [cos_low], [sin_low]
        for jump in (axis, 3 + axis):
            c, s = row_of(jump_cos, jump, 8), row_of(jump_sin, jump, 8)
            cosines.append(cos_low * c - sin_low * s)
            sines.append(sin_low * c + cos_low * s)
        tables.append((cosines, sines))
    return tables


def pair_rows(first, second):
    lanes = first[0].shape[1]
    lower = iota((8, lanes), 0) < 4

    def of(number):
        return row_of(first[number // 8], number % 8, 8)

    groups = [of(h) * second[0] for h in range(21)]
    groups += [of(h) * second[1] for h in range(19)]
    swapped = pltpu.roll(second[2], 4, 0)
    tail = jnp.where(lower, second[2], swapped)
    groups += [jnp.where(lower, of(2 * g), of(2 * g + 1)) * tail for g in range(7)]
    groups.append(of(0) * swapped)
    return groups


def pair_values(numbers):
    tail = numbers - 320
    first = jnp.where(
        numbers < 168,
        jnp.right_shift(numbers, 3),
        jnp.where(numbers < 320, jnp.right_shift(numbers - 168, 3), jnp.where(numbers < 376, jnp.right_shift(tail, 2), 0)),
    )
    second = jnp.where(
        numbers < 168,
        jnp.bitwise_and(numbers, 7),
        jnp.where(
            numbers < 320, jnp.bitwise_and(numbers, 7) + 8, jnp.where(numbers < 376, jnp.bitwise_and(tail, 3) + 16, 20)
        ),
    )
    return first, second


def fill_grid(recv_ref, device, place, grid_ref, third_ref, skipped=0):
    atoms = recv_ref.shape[2]
    tables = harmonic_tables(recv_ref[device, 0:common, :].astype(f32))
    spot = pl.ds(pl.multiple_of(place * atoms, atoms), atoms)
    third_spot = pl.ds(pl.multiple_of((place + skipped) * atoms, atoms), atoms)
    for kind in range(2):
        for piece in range(3):
            third_ref[24 * kind + 8 * piece : 24 * kind + 8 * piece + 8, third_spot] = tables[2][kind][piece]
    for kind in range(4):
        groups = pair_rows(tables[0][kind // 2], tables[1][kind % 2])
        for at in range(0, pair_groups, 2):
            start = kind * pairs + at * 8
            grid_ref[start : start + 16, spot] = jnp.concatenate(groups[at : at + 2], axis=0).astype(bf16)


def own_tables(recv_ref, sizes):
    device = lax.axis_index("dom") * sizes[1] + lax.axis_index("sub")
    return harmonic_tables(recv_ref[device, 0:common, :].astype(f32))


def own_side(recv_ref, sizes, right_ref):
    atoms = recv_ref.shape[2]
    tables = own_tables(recv_ref, sizes)
    first, second = pair_values(iota((pairs, atoms), 0))
    first, second = first.astype(f32), second.astype(f32)
    basis = [jnp.concatenate(pair_rows(tables[0][kind // 2], tables[1][kind % 2]), axis=0) for kind in range(4)]
    along_x = [-first * basis[2], -first * basis[3], first * basis[0], first * basis[1]]
    along_y = [-second * basis[1], second * basis[0], -second * basis[3], second * basis[2]]
    for d, part in enumerate((basis, along_x, along_y)):
        for kind in range(4):
            right_ref[kind * pairs : (kind + 1) * pairs, d * atoms : (d + 1) * atoms] = part[kind].astype(bf16)


def grid_kernel(sizes, recv_ref, out_ref, third_ref, right_ref, grid_ref, sems):
    chunks, _, width = out_ref.shape
    atoms = recv_ref.shape[2]
    blocks = width // atoms
    copies = [pltpu.make_async_copy(grid_ref.at[c], out_ref.at[c], sems.at[c]) for c in range(chunks)]
    for c in range(chunks):

        def one(place, carry):
            fill_grid(recv_ref, c * blocks + place, place, grid_ref.at[c], third_ref, c * blocks)
            return carry

        lax.fori_loop(0, blocks, one, 0)
        copies[c].start()
    own_side(recv_ref, sizes, right_ref)
    for copy in copies:
        copy.wait()


def make_left(sum_ref, third_ref, left_ref, latent, first_device, chunk):
    atoms = sum_ref.shape[2]

    def one(place, inner):
        spot = pl.ds(pl.multiple_of(place * atoms, atoms), atoms)
        charge = sum_ref[first_device + place, 0:latent, :].astype(f32)
        left = []
        for kind in range(2):
            for m in range(harmonics):
                left.append(charge * jnp.broadcast_to(third_ref[24 * kind + m : 24 * kind + m + 1, spot], (latent, atoms)))
        for at in range(0, 2 * harmonics, 2):
            left_ref[at * latent : (at + 2) * latent, spot] = jnp.concatenate(left[at : at + 2], axis=0).astype(bf16)
        return inner

    lax.fori_loop(0, chunk, one, 0)


def tiled_ewald_kernel(
    cells,
    total_atoms,
    sizes,
    sum_ref,
    charge_ref,
    recv_ref,
    third_ref,
    right_ref,
    grid_ref,
    pot_ref,
    force_ref,
    left_ref,
    prod_ref,
    mask_ref,
    mix_ref,
    held_ref,
    sems,
):
    chunks, total, width = grid_ref.shape
    tiles, start = [], 0
    for size in (256, 256, 512, 512):
        tiles.append((start, size))
        start += size
    copies = [
        [
            pltpu.make_async_copy(
                grid_ref.at[c, start : start + size, :],
                held_ref.at[start : start + size, c * width : (c + 1) * width],
                sems.at[number, c],
            )
            for c in range(chunks)
        ]
        for number, (start, size) in enumerate(tiles)
    ]
    for group in copies:
        for copy in group:
            copy.start()
    make_left(sum_ref, third_ref, left_ref, charge_ref.shape[0], 0, sum_ref.shape[0])
    for group, (start, size) in zip(copies, tiles, strict=True):
        for copy in group:
            copy.wait()
        prod_ref[:, start : start + size] = dot(left_ref[...], held_ref[start : start + size, :], ((1,), (1,)))
    apply_sums(cells, total_atoms, sizes, sum_ref, charge_ref, recv_ref, right_ref, pot_ref, force_ref, prod_ref, mask_ref, mix_ref)


def chunked_ewald_kernel(
    cells,
    total_atoms,
    sizes,
    sum_ref,
    charge_ref,
    recv_ref,
    pot_ref,
    force_ref,
    left_ref,
    prod_ref,
    mask_ref,
    mix_ref,
    grid_ref,
    third_ref,
    right_ref,
):
    atoms = charge_ref.shape[1]
    chunk = grid_ref.shape[1] // atoms
    own_side(recv_ref, sizes, right_ref)
    prod_ref[...] = jnp.zeros(prod_ref.shape, f32)

    def whole_chunk(number, carry):
        def one(place, inner):
            fill_grid(recv_ref, number * chunk + place, place, grid_ref, third_ref)
            return inner

        lax.fori_loop(0, chunk, one, 0)
        make_left(sum_ref, third_ref, left_ref, charge_ref.shape[0], number * chunk, chunk)

        def tile(column, inner):
            spot = pl.ds(pl.multiple_of(column * 256, 256), 256)
            prod_ref[:, spot] = prod_ref[:, spot] + dot(left_ref[...], grid_ref[spot, :], ((1,), (1,)))
            return inner

        return lax.fori_loop(0, 4 * pairs // 256, tile, carry)

    lax.fori_loop(0, sum_ref.shape[0] // chunk, whole_chunk, 0)
    apply_sums(cells, total_atoms, sizes, sum_ref, charge_ref, recv_ref, right_ref, pot_ref, force_ref, prod_ref, mask_ref, mix_ref)


def apply_sums(cells, total_atoms, sizes, sum_ref, charge_ref, recv_ref, right_ref, pot_ref, force_ref, prod_ref, mask_ref, mix_ref):
    latent, atoms = charge_ref.shape
    for device in range(-(-mask_rows // cells)):
        mask_ref[device * cells : (device + 1) * cells, :] = sum_ref[device, latent : latent + cells, :].astype(f32)
    first, second = pair_values(iota((8, pairs), 1))
    flat = (first * first + second * second).astype(f32)
    for m in range(harmonics):
        square = flat + float(m * m)
        square = jnp.maximum(square, 1.0)
        decay = jnp.exp(-smearing * square) / square
        for block in range(lane_blocks):
            factor = decay[:, block * 128 : (block + 1) * 128]

            def cell(side, third):
                row = (block * 2 + side) * signed + third + reach - 1
                return jnp.broadcast_to(mask_ref[row : row + 1, :], (8, 128)) * factor

            up = [cell(side, m) for side in range(2)]
            if 0 < m < reach:
                down = [cell(side, -m) for side in range(2)]
                upper = [up[side] + down[side] for side in range(2)]
                lower = [up[side] - down[side] for side in range(2)]
            else:
                upper = lower = up
            weight = (upper[0] + upper[1], upper[0] - upper[1], lower[0] + lower[1], lower[0] - lower[1])

            def at(u, v, w):
                row = (u * harmonics + m) * latent
                col = (v * 2 + w) * pairs + block * 128
                return slice(row, row + latent), slice(col, col + 128)

            real = (at(0, 0, 0), at(0, 1, 1), at(1, 1, 0), at(1, 0, 1))
            imag = (at(0, 1, 0), at(0, 0, 1), at(1, 0, 0), at(1, 1, 1))
            for places, signs in ((real, (1, -1, -1, -1)), (imag, (1, 1, 1, -1))):
                values = [prod_ref[place] for place in places]
                for j, place in enumerate(places):
                    mixed = None
                    for i, value in enumerate(values):
                        term = weight[i ^ j] * value
                        if mixed is None:
                            mixed = term if signs[i] == signs[j] else -term
                        else:
                            mixed = mixed + term if signs[i] == signs[j] else mixed - term
                    mix_ref[place] = mixed

    tables = own_tables(recv_ref, sizes)
    product = dot(mix_ref[...].astype(bf16), right_ref[...], ((1,), (0,)))
    potential = jnp.zeros((latent, atoms), f32)
    slopes = [jnp.zeros((latent, atoms), f32) for _ in range(3)]
    for u in range(2):
        for m in range(harmonics):
            factor = row_of(tables[2][u][m // 8], m % 8, latent)
            turned = row_of(tables[2][1 - u][m // 8], m % 8, latent) * float(m if u else -m)
            row = (u * harmonics + m) * latent
            part = [product[row : row + latent, d * atoms : (d + 1) * atoms] for d in range(3)]
            potential = potential + factor * part[0]
            slopes[0] = slopes[0] + factor * part[1]
            slopes[1] = slopes[1] + factor * part[2]
            slopes[2] = slopes[2] + turned * part[0]
    scale = 1.0 / math.sqrt(total_atoms)
    pot_ref[...] = potential * scale
    charge = charge_ref[...]
    for d in range(3):
        force_ref[d : d + 1, :] = jnp.sum(charge * slopes[d], axis=0, keepdims=True) * -scale


def vmem(count):
    return [pl.BlockSpec(memory_space=pltpu.VMEM)] * count


def per_device(
    positions,
    species,
    neighbours,
    ghost_rows,
    wavevectors,
    embedding,
    w_in,
    radial,
    norm_gain,
    w_out,
    w_charge,
):
    axes = ("dom", "sub")
    sizes = (lax.axis_size("dom"), lax.axis_size("sub"))
    count = sizes[0] * sizes[1]
    atoms = positions.shape[1]
    latent = w_charge.shape[1]
    slots = neighbours.shape[0]
    params = pltpu.CompilerParams(vmem_limit_bytes=32 * 1024 * 1024)
    outgoing = pl.pallas_call(
        functools.partial(pack_kernel, sizes),
        out_shape=jax.ShapeDtypeStruct((count, common + slots // 4, atoms), bf16),
        in_specs=vmem(4),
        out_specs=vmem(1)[0],
    )(positions, species[None, :], neighbours, ghost_rows)
    received = lax.all_to_all(outgoing, axes, 0, 0, tiled=True)
    cells = -(-mask_rows // count)
    channels = w_in.shape[1]
    bases = radial.shape[1]
    ready = pl.pallas_call(
        functools.partial(ready_kernel, sizes, cells),
        out_shape=(
            jax.ShapeDtypeStruct((2 * atoms, atoms), f32),
            jax.ShapeDtypeStruct((channels, (bases + 2) * atoms), f32),
            jax.ShapeDtypeStruct((channels, 16 * bases), f32),
            jax.ShapeDtypeStruct((3 * channels + 16, channels), bf16),
            jax.ShapeDtypeStruct((cells, atoms), f32),
            jax.ShapeDtypeStruct((slots, atoms), i32),
        ),
        in_specs=vmem(8),
        out_specs=tuple(vmem(6)),
        compiler_params=params,
    )(neighbours, wavevectors, embedding, w_in, radial, norm_gain, w_out, w_charge.T)
    rows_out = -(-(latent + cells) // 8) * 8
    outgoing, charges = pl.pallas_call(
        functools.partial(charge_kernel, sizes, cells),
        out_shape=(
            jax.ShapeDtypeStruct((count, rows_out, atoms), bf16),
            jax.ShapeDtypeStruct((latent, atoms), f32),
        ),
        in_specs=vmem(7),
        out_specs=tuple(vmem(2)),
        compiler_params=params,
    )(received, *ready)
    sums = lax.all_to_all(outgoing, axes, 0, 0, tiled=True)
    chunk = math.gcd(count, 32)
    rows = latent * 2 * harmonics
    results = (
        jax.ShapeDtypeStruct((latent, atoms), f32),
        jax.ShapeDtypeStruct((3, atoms), f32),
    )
    tables = (
        ((4 * pairs, chunk * atoms), bf16),
        ((48, chunk * atoms), f32),
        ((4 * pairs, 3 * atoms), bf16),
    )
    scratch = [
        pltpu.VMEM((rows, chunk * atoms), bf16),
        pltpu.VMEM((rows, 4 * pairs), f32),
        pltpu.VMEM((-(-mask_rows // cells) * cells, 128), f32),
        pltpu.VMEM((rows, 4 * pairs), f32),
    ]
    if chunk < count:
        return pl.pallas_call(
            functools.partial(chunked_ewald_kernel, cells, atoms * count, sizes),
            out_shape=results,
            in_specs=vmem(3),
            out_specs=tuple(vmem(2)),
            scratch_shapes=scratch + [pltpu.VMEM(*table) for table in tables],
        )(sums, charges, received)
    chunks = count // math.gcd(count, 4)
    hbm = pl.BlockSpec(memory_space=pltpu.HBM)
    grid, third, right = pl.pallas_call(
        functools.partial(grid_kernel, sizes),
        out_shape=(
            pltpu.HBM((chunks, 4 * pairs, count * atoms // chunks), bf16),
            jax.ShapeDtypeStruct(*tables[1]),
            jax.ShapeDtypeStruct(*tables[2]),
        ),
        in_specs=vmem(1),
        out_specs=(hbm, *vmem(2)),
        scratch_shapes=[
            pltpu.VMEM((chunks, 4 * pairs, count * atoms // chunks), bf16),
            pltpu.SemaphoreType.DMA((chunks,)),
        ],
        compiler_params=params,
    )(received)
    return pl.pallas_call(
        functools.partial(tiled_ewald_kernel, cells, atoms * count, sizes),
        out_shape=results,
        in_specs=vmem(5) + [hbm],
        out_specs=tuple(vmem(2)),
        scratch_shapes=scratch + [pltpu.VMEM(*tables[0]), pltpu.SemaphoreType.DMA((4, chunks))],
        compiler_params=params,
    )(sums, charges, received, third, right, pltpu.with_memory_space_constraint(grid, pltpu.HBM))


def solution(mesh):
    split = P(None, ("dom", "sub"))
    return jax.shard_map(
        per_device,
        mesh=mesh,
        in_specs=(split, P(("dom", "sub")), split, split) + (P(),) * 7,
        out_specs=(split, split),
        check_vma=False,
    )
```

```python
import functools
import math

import jax
import jax.numpy as jnp
from jax import lax
from jax.experimental import pallas as pl
from jax.experimental.pallas import tpu as pltpu
from jax.sharding import PartitionSpec as P

f32, bf16, i32 = jnp.float32, jnp.bfloat16, jnp.int32
smearing = 0.005
epsilon = 1e-05
highest = lax.Precision.HIGHEST

reach = 20
harmonics = reach + 1
signed = 2 * reach
pair_groups = 48
pairs = 8 * pair_groups
lane_blocks = pairs // 128
mask_rows = lane_blocks * 2 * signed
common = 8

sin_terms = (3.14159258, -5.16770688, 2.55003138, -0.59804517, 0.07722013)
cos_terms = (0.99999995, -4.93479286, 4.05841191, -1.33188016, 0.21969679)
sends = ((1, 0), (-1, 0), (0, 1), (0, -1))
ghost_order = (1, 0, 3, 2)


def poly(terms, square):
    total = jnp.full_like(square, terms[-1])
    for term in terms[-2::-1]:
        total = total * square + term
    return total


def sin_pi(turns):
    rest = turns - jnp.round(turns)
    return rest * poly(sin_terms, rest * rest)


def cos_sin(turns):
    rest = turns - jnp.round(turns)
    square = rest * rest
    half_sin = rest * poly(sin_terms, square)
    half_cos = poly(cos_terms, square)
    return 1.0 - 2.0 * half_sin * half_sin, 2.0 * half_sin * half_cos


def iota(shape, axis):
    return lax.broadcasted_iota(i32, shape, axis)


def lanes_of(shape, width):
    return lax.div(iota(shape, len(shape) - 1), jnp.int32(width))


def by_block(parts, width):
    which = lanes_of(parts[0].shape, width)
    out = parts[-1]
    for number in range(len(parts) - 2, -1, -1):
        out = jnp.where(which == number, parts[number], out)
    return out


def row_of(values, row, count):
    return jnp.broadcast_to(values[row : row + 1], (count,) + values.shape[1:])


def take_lanes(row_values, index):
    return jnp.take_along_axis(row_values, index, axis=1)


def dot(left, right, dims, precision=None):
    return lax.dot_general(left, right, ((dims[0], dims[1]), ((), ())), precision=precision, preferred_element_type=f32)


def pack_kernel(sizes, pos_ref, spec_ref, nbr_ref, rows_ref, out_ref):
    n_dom, n_sub = sizes
    count, _, atoms = out_ref.shape
    ghosts = rows_ref.shape[1]
    slots = nbr_ref.shape[0]
    quarter = slots // 4
    order = jnp.concatenate([rows_ref[row : row + 1, :] for row in ghost_order], axis=1)
    head = jnp.concatenate(
        [
            pos_ref[...].astype(f32),
            spec_ref[...].astype(f32),
            order.astype(f32),
            jnp.zeros((common - 5, atoms), f32),
        ],
        axis=0,
    )
    whole = jnp.concatenate([head, jnp.zeros((quarter, atoms), f32)], axis=0).astype(bf16)
    for device in range(count):
        out_ref[device] = whole
    index = jnp.broadcast_to(order, (8, atoms))
    lists = [take_lanes(nbr_ref[8 * s : 8 * s + 8, :], index).astype(f32) for s in range(slots // 8)]
    per = quarter // 8
    dom, sub = lax.axis_index("dom"), lax.axis_index("sub")
    for block, (dom_step, sub_step) in enumerate(sends):
        rows = []
        for piece in range(per):
            parts = [
                pltpu.roll(lists[r * per + piece], (ghosts * (r - block)) % atoms, 1) if r != block else lists[r * per + piece]
                for r in range(4)
            ]
            rows.append(by_block(parts, ghosts))
        target = lax.rem(dom + dom_step + n_dom, n_dom) * n_sub + lax.rem(sub + sub_step + n_sub, n_sub)
        out_ref[target, common:, :] = jnp.concatenate(rows, axis=0).astype(bf16)


def first_layer_sums(lists, tables, centre, ghosts, bases):
    total = [[None] * bases for _ in range(2)]
    for listed in lists:
        index = jnp.maximum(listed, 0)
        low = jnp.bitwise_and(index, 127)
        is_ghost = index >= 128
        found = []
        for quantity in range(4):
            parts = [
                jnp.where(is_ghost, take_lanes(row_of(outer, quantity, 8), low), take_lanes(row_of(inner, quantity, 8), low))
                for inner, outer in tables
            ]
            found.append(by_block(parts, ghosts) if len(parts) > 1 else parts[0])
        chord = jnp.zeros(low.shape, f32)
        for axis in range(3):
            wave = sin_pi(found[axis] - row_of(centre, axis, 8))
            chord = chord + wave * wave
        first = jnp.where(listed >= 0, jnp.exp(-0.125 * chord), 0.0)
        for kind in range(2):
            power = jnp.where((found[3] > 0.5) if kind else (found[3] <= 0.5), first, 0.0)
            for basis in range(bases):
                if basis:
                    power = power * power
                total[kind][basis] = power if total[kind][basis] is None else total[kind][basis] + power
    return jnp.concatenate(total[0] + total[1], axis=0)


def wave_mask(wave_ref):
    first = wave_ref[0:1, :]
    second = wave_ref[1:2, :]
    third = wave_ref[2:3, :]
    size = jnp.abs(second)
    pair = jnp.where(
        size < 8,
        8 * first + size,
        jnp.where(size < 16, 160 + 8 * first + size, jnp.where(size < 20, 304 + 4 * first + size, 376)),
    )
    side = jnp.where(second < 0, 1, 0)
    row = (jnp.right_shift(pair, 7) * 2 + side) * signed + third + (reach - 1)
    lane = jnp.bitwise_and(pair, 127)
    total_k = row.shape[1]
    left = jnp.where(iota((mask_rows, total_k), 0) == row, 1.0, 0.0).astype(bf16)
    right = jnp.where(iota((128, total_k), 0) == lane, 1.0, 0.0).astype(bf16)
    return dot(left, right, ((1,), (1,)))


def normed_silu(message, gain):
    normed = message * lax.rsqrt(jnp.mean(message * message, axis=0, keepdims=True) + epsilon) * gain
    return (normed / (1.0 + jnp.exp(-normed))).astype(bf16)


def ready_kernel(nbr_ref, emb_ref, w_in_ref, radial_ref, gain_ref, w_out_ref, w_charge_ref, times_ref, column_ref, weight_ref, turned_ref, list_ref):
    atoms = nbr_ref.shape[1]
    slots = nbr_ref.shape[0]
    bases = radial_ref.shape[1]
    channels = w_in_ref.shape[1]
    latent = w_charge_ref.shape[0]

    kinds = jnp.concatenate([emb_ref[...].astype(f32), jnp.zeros((6, channels), f32)], axis=0).astype(bf16)
    two_feats = dot(kinds, w_in_ref[0], ((1,), (0,))).astype(bf16).astype(f32)
    radial_first = radial_ref[0].astype(f32)
    weights = jnp.concatenate(
        [
            jnp.broadcast_to(radial_first[basis : basis + 1] * two_feats[kind : kind + 1], (8, channels))
            for kind in range(2)
            for basis in range(bases)
        ],
        axis=0,
    )
    weight_ref[...] = weights.T
    params = jnp.concatenate(
        [radial_ref[1].astype(f32), gain_ref[...].astype(f32), jnp.zeros((16 - bases - 2, channels), f32)], axis=0
    ).astype(bf16)
    width = column_ref.shape[1]
    spread = jnp.where(iota((16, width), 0) == lanes_of((16, width), atoms), 1.0, 0.0).astype(bf16)
    column_ref[...] = dot(params, spread, ((0,), (0,)))
    for place, weight in enumerate((w_out_ref[0], w_in_ref[1], w_out_ref[1])):
        turned_ref[place * channels : (place + 1) * channels, :] = weight.astype(f32).T.astype(bf16)
    turned_ref[3 * channels : 3 * channels + 16, :] = jnp.concatenate(
        [w_charge_ref[...].astype(f32), emb_ref[...].astype(f32), jnp.zeros((16 - 2 - latent, channels), f32)], axis=0
    ).astype(bf16)
    listed = [nbr_ref[8 * s : 8 * s + 8, :].astype(f32) for s in range(slots // 8)]
    for half in range(2):
        row_number = (iota((atoms, atoms), 0) + half * atoms).astype(f32)
        times = jnp.zeros((atoms, atoms), f32)
        for slot in range(slots):
            times = times + jnp.where(row_number == row_of(listed[slot // 8], slot % 8, atoms), 1.0, 0.0)
        times_ref[half * atoms : (half + 1) * atoms, :] = times
    list_ref[...] = nbr_ref[...]


def charge_kernel(
    sizes,
    recv_ref,
    times_ref,
    column_ref,
    weight_ref,
    turned_ref,
    nbr_ref,
    out_ref,
    charge_ref,
):
    n_dom, n_sub = sizes
    count = out_ref.shape[0]
    atoms = nbr_ref.shape[1]
    slots = nbr_ref.shape[0]
    channels = column_ref.shape[0]
    bases = column_ref.shape[1] // atoms - 2
    latent = charge_ref.shape[0]
    ghosts = atoms // 4
    quarter = slots // 4
    dom, sub = lax.axis_index("dom"), lax.axis_index("sub")

    def device_at(dom_step, sub_step):
        return lax.rem(dom + dom_step + 2 * n_dom, n_dom) * n_sub + lax.rem(sub + sub_step + 2 * n_sub, n_sub)

    origins = tuple((-dom_step, -sub_step) for dom_step, sub_step in sends)
    data, picked = {}, {}
    for base in ((0, 0),) + origins:
        for step in ((0, 0),) + origins:
            key = (base[0] + step[0], base[1] + step[1])
            if key not in data:
                data[key] = recv_ref[device_at(*key), 0:common, :].astype(f32)
                index = row_of(data[key], 4, common).astype(i32)
                picked[key] = take_lanes(data[key], index)

    def table(key):
        return data[key], by_block([picked[(key[0] + s[0], key[1] + s[1])] for s in origins], ghosts)

    own = data[(0, 0)]
    own_table = table((0, 0))
    own_ghosts = own_table[1]

    own_lists = [nbr_ref[8 * s : 8 * s + 8, :] for s in range(slots // 8)]
    sent = [recv_ref[device_at(*key), common:, :].astype(f32) for key in origins]
    ghost_lists = []
    for r in range(4):
        for piece in range(quarter // 8):
            parts = []
            for block in range(4):
                part = sent[block][8 * piece : 8 * piece + 8]
                shift = (ghosts * (block - r)) % atoms
                parts.append(pltpu.roll(part, shift, 1) if shift else part)
            ghost_lists.append(by_block(parts, ghosts).astype(i32))

    sums = jnp.concatenate(
        [
            first_layer_sums(own_lists, [own_table], own, ghosts, bases),
            first_layer_sums(ghost_lists, [table(key) for key in origins], own_ghosts, ghosts, bases),
        ],
        axis=1,
    )
    message = dot(weight_ref[...], sums, ((1,), (0,)), highest)

    def column(number):
        return column_ref[:, number * atoms : (number + 1) * atoms]

    def turned(place):
        return turned_ref[place * channels : (place + 1) * channels, :]

    gain_first = column(bases)
    activated = normed_silu(message, jnp.concatenate([gain_first, gain_first], axis=1))
    species = jnp.concatenate([own[3:4], own_ghosts[3:4]], axis=1)
    kind_rows = iota((16, 2 * atoms), 0) - latent
    choice = jnp.where(jnp.where(species > 0.5, 1, 0) == kind_rows, 1.0, 0.0).astype(bf16)
    last = turned_ref[3 * channels : 3 * channels + 16, :]
    hidden = dot(last, choice, ((0,), (0,)))
    hidden = (hidden + dot(turned(0), activated, ((1,), (0,)))).astype(bf16)
    feats = dot(turned(1), hidden, ((1,), (0,))).astype(bf16)

    cosines, sines = cos_sin(jnp.concatenate([own, own_ghosts], axis=1))
    is_axis = iota((8, 2 * atoms), 0) < 3
    waves = jnp.concatenate([jnp.where(is_axis, cosines, 0.0), jnp.where(is_axis, sines, 0.0)], axis=0)
    chord = 1.5 - 0.5 * dot(waves, waves[:, :atoms], ((0,), (0,)), highest)
    times = times_ref[...]
    power = jnp.exp(-0.125 * chord)
    message = jnp.zeros((channels, atoms), f32)
    for basis in range(bases):
        if basis:
            power = power * power
        weighted = times * power
        high = weighted.astype(bf16)
        low = (weighted - high.astype(f32)).astype(bf16)
        mixed = dot(feats, high, ((1,), (0,))) + dot(feats, low, ((1,), (0,)))
        message = message + column(basis) * mixed
    activated = normed_silu(message, column(bases + 1))
    hidden = (hidden[:, :atoms].astype(f32) + dot(turned(2), activated, ((1,), (0,)))).astype(bf16)
    charges = dot(last, hidden, ((1,), (0,)))[:latent]
    charge_ref[...] = charges
    block = charges.astype(bf16)
    for device in range(count):
        out_ref[device] = block


def harmonic_tables(coords):
    lanes = coords.shape[1]
    step = iota((8, lanes), 0)
    big = jnp.where(step < 3, 8.0, 16.0)
    far = jnp.concatenate([coords[0:3], coords[0:3], coords[0:2]], axis=0)
    jump_cos, jump_sin = cos_sin(big * far)
    tables = []
    for axis in range(3):
        cos_low, sin_low = cos_sin(step.astype(f32) * row_of(coords, axis, 8))
        cosines, sines = [cos_low], [sin_low]
        for jump in (axis, 3 + axis):
            c, s = row_of(jump_cos, jump, 8), row_of(jump_sin, jump, 8)
            cosines.append(cos_low * c - sin_low * s)
            sines.append(sin_low * c + cos_low * s)
        tables.append((cosines, sines))
    return tables


def pair_rows(first, second):
    lanes = first[0].shape[1]
    lower = iota((8, lanes), 0) < 4

    def of(number):
        return row_of(first[number // 8], number % 8, 8)

    groups = [of(h) * second[0] for h in range(21)]
    groups += [of(h) * second[1] for h in range(19)]
    swapped = pltpu.roll(second[2], 4, 0)
    tail = jnp.where(lower, second[2], swapped)
    groups += [jnp.where(lower, of(2 * g), of(2 * g + 1)) * tail for g in range(7)]
    groups.append(of(0) * swapped)
    return groups


def pair_values(numbers):
    tail = numbers - 320
    first = jnp.where(
        numbers < 168,
        jnp.right_shift(numbers, 3),
        jnp.where(numbers < 320, jnp.right_shift(numbers - 168, 3), jnp.where(numbers < 376, jnp.right_shift(tail, 2), 0)),
    )
    second = jnp.where(
        numbers < 168,
        jnp.bitwise_and(numbers, 7),
        jnp.where(
            numbers < 320, jnp.bitwise_and(numbers, 7) + 8, jnp.where(numbers < 376, jnp.bitwise_and(tail, 3) + 16, 20)
        ),
    )
    return first, second


def fill_products(first, second, kinds, spot, grid_ref):
    for kind in kinds:
        groups = pair_rows(first[kind // 2], second[kind % 2])
        for at in range(0, pair_groups, 2):
            start = (kind * pair_groups + at) * 8
            grid_ref[start : start + 16, spot] = jnp.concatenate(groups[at : at + 2], axis=0).astype(bf16)


def fill_grid(recv_ref, device, place, grid_ref, third_ref, kinds, skipped=0, flat_ref=None):
    atoms = recv_ref.shape[2]
    tables = harmonic_tables(recv_ref[device, 0:common, :].astype(f32))
    spot = pl.ds(pl.multiple_of(place * atoms, atoms), atoms)
    later = pl.ds(pl.multiple_of((place + skipped) * atoms, atoms), atoms)
    for kind in range(2):
        for piece in range(3):
            third_ref[24 * kind + 8 * piece : 24 * kind + 8 * piece + 8, later] = tables[2][kind][piece]
    if flat_ref is not None:
        for number, table in enumerate((tables[0][1], tables[1][0], tables[1][1])):
            for piece in range(3):
                flat_ref[24 * number + 8 * piece : 24 * number + 8 * piece + 8, later] = table[piece]
    fill_products(tables[0], tables[1], kinds, spot, grid_ref)


def own_tables(recv_ref, sizes):
    device = lax.axis_index("dom") * sizes[1] + lax.axis_index("sub")
    return harmonic_tables(recv_ref[device, 0:common, :].astype(f32))


def own_side(recv_ref, sizes, right_ref):
    atoms = recv_ref.shape[2]
    tables = own_tables(recv_ref, sizes)
    first, second = pair_values(iota((pairs, atoms), 0))
    first, second = first.astype(f32), second.astype(f32)
    basis = [jnp.concatenate(pair_rows(tables[0][kind // 2], tables[1][kind % 2]), axis=0) for kind in range(4)]
    along_x = [-first * basis[2], -first * basis[3], first * basis[0], first * basis[1]]
    along_y = [-second * basis[1], second * basis[0], -second * basis[3], second * basis[2]]
    for d, part in enumerate((basis, along_x, along_y)):
        for kind in range(4):
            right_ref[kind * pairs : (kind + 1) * pairs, d * atoms : (d + 1) * atoms] = part[kind].astype(bf16)


def grid_kernel(sizes, recv_ref, wave_ref, out_ref, side_ref, third_ref, flat_ref, mask_ref, grid_ref, right_ref, sems):
    chunks, _, width = out_ref.shape
    atoms = recv_ref.shape[2]
    blocks = width // atoms
    copies = [pltpu.make_async_copy(grid_ref.at[c], out_ref.at[c], sems.at[c]) for c in range(chunks)]
    copies.append(pltpu.make_async_copy(right_ref, side_ref, sems.at[chunks]))
    own_side(recv_ref, sizes, right_ref)
    copies[chunks].start()
    for c in range(chunks):

        def one(place, carry):
            fill_grid(recv_ref, c * blocks + place, place, grid_ref.at[c], third_ref, (0, 1), c * blocks, flat_ref)
            return carry

        lax.fori_loop(0, blocks, one, 0)
        copies[c].start()
    mask_ref[...] = wave_mask(wave_ref)
    for copy in copies:
        copy.wait()


def make_left(sum_ref, third_ref, left_ref, latent, first_device, chunk):
    atoms = sum_ref.shape[2]

    def one(place, inner):
        spot = pl.ds(pl.multiple_of(place * atoms, atoms), atoms)
        charge = sum_ref[first_device + place, 0:latent, :].astype(f32)
        left = []
        for kind in range(2):
            for m in range(harmonics):
                left.append(charge * jnp.broadcast_to(third_ref[24 * kind + m : 24 * kind + m + 1, spot], (latent, atoms)))
        for at in range(0, 2 * harmonics, 2):
            left_ref[at * latent : (at + 2) * latent, spot] = jnp.concatenate(left[at : at + 2], axis=0).astype(bf16)
        return inner

    lax.fori_loop(0, chunk, one, 0)


def tiled_ewald_kernel(
    total_atoms,
    sizes,
    sum_ref,
    charge_ref,
    recv_ref,
    third_ref,
    flat_ref,
    mask_ref,
    side_ref,
    grid_ref,
    pot_ref,
    force_ref,
    left_ref,
    prod_ref,
    mix_ref,
    held_ref,
    right_ref,
    sems,
):
    chunks, half, width = grid_ref.shape
    atoms = recv_ref.shape[2]
    copies = [
        pltpu.make_async_copy(grid_ref.at[c], held_ref.at[0:half, c * width : (c + 1) * width], sems.at[c])
        for c in range(chunks)
    ]
    copies.append(pltpu.make_async_copy(side_ref, right_ref, sems.at[chunks]))
    for copy in copies:
        copy.start()
    make_left(sum_ref, third_ref, left_ref, charge_ref.shape[0], 0, sum_ref.shape[0])

    def one(place, carry):
        spot = pl.ds(pl.multiple_of(place * atoms, atoms), atoms)
        x_sin, y_cos, y_sin = (
            [flat_ref[24 * number + 8 * piece : 24 * number + 8 * piece + 8, spot] for piece in range(3)]
            for number in range(3)
        )
        fill_products((None, x_sin), (y_cos, y_sin), (2, 3), spot, held_ref)
        return carry

    lax.fori_loop(0, sum_ref.shape[0], one, 0)
    for copy in copies:
        copy.wait()
    prod_ref[...] = dot(left_ref[...], held_ref[...], ((1,), (1,)))
    apply_sums(total_atoms, sizes, charge_ref, recv_ref, right_ref, pot_ref, force_ref, prod_ref, mask_ref, mix_ref)


def chunked_ewald_kernel(
    total_atoms,
    sizes,
    sum_ref,
    charge_ref,
    recv_ref,
    wave_ref,
    pot_ref,
    force_ref,
    left_ref,
    prod_ref,
    mix_ref,
    grid_ref,
    third_ref,
    right_ref,
    mask_ref,
):
    atoms = charge_ref.shape[1]
    chunk = grid_ref.shape[1] // atoms
    own_side(recv_ref, sizes, right_ref)
    prod_ref[...] = jnp.zeros(prod_ref.shape, f32)
    mask_ref[...] = wave_mask(wave_ref)

    def whole_chunk(number, carry):
        def one(place, inner):
            fill_grid(recv_ref, number * chunk + place, place, grid_ref, third_ref, range(4))
            return inner

        lax.fori_loop(0, chunk, one, 0)
        make_left(sum_ref, third_ref, left_ref, charge_ref.shape[0], number * chunk, chunk)

        def tile(column, inner):
            spot = pl.ds(pl.multiple_of(column * 256, 256), 256)
            prod_ref[:, spot] = prod_ref[:, spot] + dot(left_ref[...], grid_ref[spot, :], ((1,), (1,)))
            return inner

        return lax.fori_loop(0, 4 * pairs // 256, tile, carry)

    lax.fori_loop(0, sum_ref.shape[0] // chunk, whole_chunk, 0)
    apply_sums(total_atoms, sizes, charge_ref, recv_ref, right_ref, pot_ref, force_ref, prod_ref, mask_ref, mix_ref)


def apply_sums(total_atoms, sizes, charge_ref, recv_ref, right_ref, pot_ref, force_ref, prod_ref, mask_ref, mix_ref):
    latent, atoms = charge_ref.shape
    first, second = pair_values(iota((8, pairs), 1))
    flat = (first * first + second * second).astype(f32)
    for m in range(harmonics):
        square = flat + float(m * m)
        square = jnp.maximum(square, 1.0)
        decay = jnp.exp(-smearing * square) / square
        for block in range(lane_blocks):
            factor = decay[:, block * 128 : (block + 1) * 128]

            def cell(side, third):
                row = (block * 2 + side) * signed + third + reach - 1
                return jnp.broadcast_to(mask_ref[row : row + 1, :], (8, 128)) * factor

            up = [cell(side, m) for side in range(2)]
            if 0 < m < reach:
                down = [cell(side, -m) for side in range(2)]
                upper = [up[side] + down[side] for side in range(2)]
                lower = [up[side] - down[side] for side in range(2)]
            else:
                upper = lower = up
            weight = (upper[0] + upper[1], upper[0] - upper[1], lower[0] + lower[1], lower[0] - lower[1])

            def at(u, v, w):
                row = (u * harmonics + m) * latent
                col = (v * 2 + w) * pairs + block * 128
                return slice(row, row + latent), slice(col, col + 128)

            real = (at(0, 0, 0), at(0, 1, 1), at(1, 1, 0), at(1, 0, 1))
            imag = (at(0, 1, 0), at(0, 0, 1), at(1, 0, 0), at(1, 1, 1))
            for places, signs in ((real, (1, -1, -1, -1)), (imag, (1, 1, 1, -1))):
                values = [prod_ref[place] for place in places]
                for j, place in enumerate(places):
                    mixed = None
                    for i, value in enumerate(values):
                        term = weight[i ^ j] * value
                        if mixed is None:
                            mixed = term if signs[i] == signs[j] else -term
                        else:
                            mixed = mixed + term if signs[i] == signs[j] else mixed - term
                    mix_ref[place] = mixed

    tables = own_tables(recv_ref, sizes)
    product = dot(mix_ref[...].astype(bf16), right_ref[...], ((1,), (0,)))
    potential = jnp.zeros((latent, atoms), f32)
    slopes = [jnp.zeros((latent, atoms), f32) for _ in range(3)]
    for u in range(2):
        for m in range(harmonics):
            factor = row_of(tables[2][u][m // 8], m % 8, latent)
            turned = row_of(tables[2][1 - u][m // 8], m % 8, latent) * float(m if u else -m)
            row = (u * harmonics + m) * latent
            part = [product[row : row + latent, d * atoms : (d + 1) * atoms] for d in range(3)]
            potential = potential + factor * part[0]
            slopes[0] = slopes[0] + factor * part[1]
            slopes[1] = slopes[1] + factor * part[2]
            slopes[2] = slopes[2] + turned * part[0]
    scale = 1.0 / math.sqrt(total_atoms)
    pot_ref[...] = potential * scale
    charge = charge_ref[...]
    for d in range(3):
        force_ref[d : d + 1, :] = jnp.sum(charge * slopes[d], axis=0, keepdims=True) * -scale


def vmem(count):
    return [pl.BlockSpec(memory_space=pltpu.VMEM)] * count


def per_device(
    positions,
    species,
    neighbours,
    ghost_rows,
    wavevectors,
    embedding,
    w_in,
    radial,
    norm_gain,
    w_out,
    w_charge,
):
    axes = ("dom", "sub")
    sizes = (lax.axis_size("dom"), lax.axis_size("sub"))
    count = sizes[0] * sizes[1]
    atoms = positions.shape[1]
    latent = w_charge.shape[1]
    slots = neighbours.shape[0]
    params = pltpu.CompilerParams(vmem_limit_bytes=32 * 1024 * 1024)
    outgoing = pl.pallas_call(
        functools.partial(pack_kernel, sizes),
        out_shape=jax.ShapeDtypeStruct((count, common + slots // 4, atoms), bf16),
        in_specs=vmem(4),
        out_specs=vmem(1)[0],
    )(positions, species[None, :], neighbours, ghost_rows)
    received = lax.all_to_all(outgoing, axes, 0, 0, tiled=True)
    channels = w_in.shape[1]
    bases = radial.shape[1]
    ready = pl.pallas_call(
        ready_kernel,
        out_shape=(
            jax.ShapeDtypeStruct((2 * atoms, atoms), f32),
            jax.ShapeDtypeStruct((channels, (bases + 2) * atoms), f32),
            jax.ShapeDtypeStruct((channels, 16 * bases), f32),
            jax.ShapeDtypeStruct((3 * channels + 16, channels), bf16),
            jax.ShapeDtypeStruct((slots, atoms), i32),
        ),
        in_specs=vmem(7),
        out_specs=tuple(vmem(5)),
        compiler_params=params,
    )(neighbours, embedding, w_in, radial, norm_gain, w_out, w_charge.T)
    outgoing, charges = pl.pallas_call(
        functools.partial(charge_kernel, sizes),
        out_shape=(
            jax.ShapeDtypeStruct((count, latent, atoms), bf16),
            jax.ShapeDtypeStruct((latent, atoms), f32),
        ),
        in_specs=vmem(6),
        out_specs=tuple(vmem(2)),
        compiler_params=params,
    )(received, *ready)
    sums = lax.all_to_all(outgoing, axes, 0, 0, tiled=True)
    chunk = math.gcd(count, 32)
    rows = latent * 2 * harmonics
    results = (
        jax.ShapeDtypeStruct((latent, atoms), f32),
        jax.ShapeDtypeStruct((3, atoms), f32),
    )
    tables = (
        ((4 * pairs, chunk * atoms), bf16),
        ((48, chunk * atoms), f32),
        ((4 * pairs, 3 * atoms), bf16),
    )
    scratch = [
        pltpu.VMEM((rows, chunk * atoms), bf16),
        pltpu.VMEM((rows, 4 * pairs), f32),
        pltpu.VMEM((rows, 4 * pairs), f32),
    ]
    if chunk < count:
        return pl.pallas_call(
            functools.partial(chunked_ewald_kernel, atoms * count, sizes),
            out_shape=results,
            in_specs=vmem(4),
            out_specs=tuple(vmem(2)),
            scratch_shapes=scratch + [pltpu.VMEM(*table) for table in tables] + [pltpu.VMEM((mask_rows, 128), f32)],
        )(sums, charges, received, wavevectors)
    chunks = count // math.gcd(count, 4)
    hbm = pl.BlockSpec(memory_space=pltpu.HBM)
    grid_shape = (chunks, 2 * pairs, count * atoms // chunks)
    grid, side, third, flat, mask = pl.pallas_call(
        functools.partial(grid_kernel, sizes),
        out_shape=(
            pltpu.HBM(grid_shape, bf16),
            pltpu.HBM(*tables[2]),
            jax.ShapeDtypeStruct(*tables[1]),
            jax.ShapeDtypeStruct((72, count * atoms), f32),
            jax.ShapeDtypeStruct((mask_rows, 128), f32),
        ),
        in_specs=vmem(2),
        out_specs=(hbm, hbm, *vmem(3)),
        scratch_shapes=[
            pltpu.VMEM(grid_shape, bf16),
            pltpu.VMEM(*tables[2]),
            pltpu.SemaphoreType.DMA((chunks + 1,)),
        ],
        compiler_params=params,
    )(received, wavevectors)
    return pl.pallas_call(
        functools.partial(tiled_ewald_kernel, atoms * count, sizes),
        out_shape=results,
        in_specs=vmem(6) + [hbm, hbm],
        out_specs=tuple(vmem(2)),
        scratch_shapes=scratch
        + [pltpu.VMEM(*tables[0]), pltpu.VMEM(*tables[2]), pltpu.SemaphoreType.DMA((chunks + 1,))],
        compiler_params=params,
    )(
        sums,
        charges,
        received,
        third,
        flat,
        mask,
        pltpu.with_memory_space_constraint(side, pltpu.HBM),
        pltpu.with_memory_space_constraint(grid, pltpu.HBM),
    )


def solution(mesh):
    split = P(None, ("dom", "sub"))
    return jax.shard_map(
        per_device,
        mesh=mesh,
        in_specs=(split, P(("dom", "sub")), split, split) + (P(),) * 7,
        out_specs=(split, split),
        check_vma=False,
    )
```

```python
import functools
import math

import jax
import jax.numpy as jnp
from jax import lax
from jax.experimental import pallas as pl
from jax.experimental.pallas import tpu as pltpu
from jax.sharding import PartitionSpec as P

f32, bf16, i32 = jnp.float32, jnp.bfloat16, jnp.int32
smearing = 0.005
epsilon = 1e-05
highest = lax.Precision.HIGHEST

reach = 20
harmonics = reach + 1
signed = 2 * reach
pair_groups = 48
pairs = 8 * pair_groups
lane_blocks = pairs // 128
mask_rows = lane_blocks * 2 * signed
common = 8

sin_terms = (3.14159258, -5.16770688, 2.55003138, -0.59804517, 0.07722013)
cos_terms = (0.99999995, -4.93479286, 4.05841191, -1.33188016, 0.21969679)
sends = ((1, 0), (-1, 0), (0, 1), (0, -1))
ghost_order = (1, 0, 3, 2)


def poly(terms, square):
    total = jnp.full_like(square, terms[-1])
    for term in terms[-2::-1]:
        total = total * square + term
    return total


def sin_pi(turns):
    rest = turns - jnp.round(turns)
    return rest * poly(sin_terms, rest * rest)


def cos_sin(turns):
    rest = turns - jnp.round(turns)
    square = rest * rest
    half_sin = rest * poly(sin_terms, square)
    half_cos = poly(cos_terms, square)
    return 1.0 - 2.0 * half_sin * half_sin, 2.0 * half_sin * half_cos


def iota(shape, axis):
    return lax.broadcasted_iota(i32, shape, axis)


def lanes_of(shape, width):
    return lax.div(iota(shape, len(shape) - 1), jnp.int32(width))


def by_block(parts, width):
    which = lanes_of(parts[0].shape, width)
    out = parts[-1]
    for number in range(len(parts) - 2, -1, -1):
        out = jnp.where(which == number, parts[number], out)
    return out


def row_of(values, row, count):
    return jnp.broadcast_to(values[row : row + 1], (count,) + values.shape[1:])


def take_lanes(row_values, index):
    return jnp.take_along_axis(row_values, index, axis=1)


def dot(left, right, dims, precision=None):
    return lax.dot_general(left, right, ((dims[0], dims[1]), ((), ())), precision=precision, preferred_element_type=f32)


def pack_kernel(sizes, pos_ref, spec_ref, nbr_ref, rows_ref, out_ref):
    n_dom, n_sub = sizes
    count, _, atoms = out_ref.shape
    ghosts = rows_ref.shape[1]
    slots = nbr_ref.shape[0]
    quarter = slots // 4
    order = jnp.concatenate([rows_ref[row : row + 1, :] for row in ghost_order], axis=1)
    head = jnp.concatenate(
        [
            pos_ref[...].astype(f32),
            spec_ref[...].astype(f32),
            order.astype(f32),
            jnp.zeros((common - 5, atoms), f32),
        ],
        axis=0,
    )
    whole = jnp.concatenate([head, jnp.zeros((quarter, atoms), f32)], axis=0).astype(bf16)
    for device in range(count):
        out_ref[device] = whole
    index = jnp.broadcast_to(order, (8, atoms))
    lists = [take_lanes(nbr_ref[8 * s : 8 * s + 8, :], index).astype(f32) for s in range(slots // 8)]
    per = quarter // 8
    dom, sub = lax.axis_index("dom"), lax.axis_index("sub")
    for block, (dom_step, sub_step) in enumerate(sends):
        rows = []
        for piece in range(per):
            parts = [
                pltpu.roll(lists[r * per + piece], (ghosts * (r - block)) % atoms, 1) if r != block else lists[r * per + piece]
                for r in range(4)
            ]
            rows.append(by_block(parts, ghosts))
        target = lax.rem(dom + dom_step + n_dom, n_dom) * n_sub + lax.rem(sub + sub_step + n_sub, n_sub)
        out_ref[target, common:, :] = jnp.concatenate(rows, axis=0).astype(bf16)


def first_layer_sums(lists, tables, centre, ghosts, bases):
    total = [[None] * bases for _ in range(2)]
    for listed in lists:
        index = jnp.maximum(listed, 0)
        low = jnp.bitwise_and(index, 127)
        is_ghost = index >= 128
        found = []
        for quantity in range(4):
            parts = [
                jnp.where(is_ghost, take_lanes(row_of(outer, quantity, 8), low), take_lanes(row_of(inner, quantity, 8), low))
                for inner, outer in tables
            ]
            found.append(by_block(parts, ghosts) if len(parts) > 1 else parts[0])
        chord = jnp.zeros(low.shape, f32)
        for axis in range(3):
            wave = sin_pi(found[axis] - row_of(centre, axis, 8))
            chord = chord + wave * wave
        first = jnp.where(listed >= 0, jnp.exp(-0.125 * chord), 0.0)
        for kind in range(2):
            power = jnp.where((found[3] > 0.5) if kind else (found[3] <= 0.5), first, 0.0)
            for basis in range(bases):
                if basis:
                    power = power * power
                total[kind][basis] = power if total[kind][basis] is None else total[kind][basis] + power
    return jnp.concatenate(total[0] + total[1], axis=0)


def wave_mask(wave_ref):
    first = wave_ref[0:1, :]
    second = wave_ref[1:2, :]
    third = wave_ref[2:3, :]
    size = jnp.abs(second)
    pair = jnp.where(
        size < 8,
        8 * first + size,
        jnp.where(size < 16, 160 + 8 * first + size, jnp.where(size < 20, 304 + 4 * first + size, 376)),
    )
    side = jnp.where(second < 0, 1, 0)
    row = (jnp.right_shift(pair, 7) * 2 + side) * signed + third + (reach - 1)
    lane = jnp.bitwise_and(pair, 127)
    total_k = row.shape[1]
    left = jnp.where(iota((mask_rows, total_k), 0) == row, 1.0, 0.0).astype(bf16)
    right = jnp.where(iota((128, total_k), 0) == lane, 1.0, 0.0).astype(bf16)
    return dot(left, right, ((1,), (1,)))


def normed_silu(message, gain):
    normed = message * lax.rsqrt(jnp.mean(message * message, axis=0, keepdims=True) + epsilon) * gain
    return (normed / (1.0 + jnp.exp(-normed))).astype(bf16)


def ready_kernel(nbr_ref, emb_ref, w_in_ref, radial_ref, gain_ref, w_out_ref, w_charge_ref, times_ref, column_ref, weight_ref, turned_ref, list_ref):
    atoms = nbr_ref.shape[1]
    slots = nbr_ref.shape[0]
    bases = radial_ref.shape[1]
    channels = w_in_ref.shape[1]
    latent = w_charge_ref.shape[0]

    kinds = jnp.concatenate([emb_ref[...].astype(f32), jnp.zeros((6, channels), f32)], axis=0).astype(bf16)
    two_feats = dot(kinds, w_in_ref[0], ((1,), (0,))).astype(bf16).astype(f32)
    radial_first = radial_ref[0].astype(f32)
    weights = jnp.concatenate(
        [
            jnp.broadcast_to(radial_first[basis : basis + 1] * two_feats[kind : kind + 1], (8, channels))
            for kind in range(2)
            for basis in range(bases)
        ],
        axis=0,
    )
    weight_ref[...] = weights.T
    params = jnp.concatenate(
        [radial_ref[1].astype(f32), gain_ref[...].astype(f32), jnp.zeros((16 - bases - 2, channels), f32)], axis=0
    ).astype(bf16)
    width = column_ref.shape[1]
    spread = jnp.where(iota((16, width), 0) == lanes_of((16, width), atoms), 1.0, 0.0).astype(bf16)
    column_ref[...] = dot(params, spread, ((0,), (0,)))
    for place, weight in enumerate((w_out_ref[0], w_in_ref[1], w_out_ref[1])):
        turned_ref[place * channels : (place + 1) * channels, :] = weight.astype(f32).T.astype(bf16)
    turned_ref[3 * channels : 3 * channels + 16, :] = jnp.concatenate(
        [w_charge_ref[...].astype(f32), emb_ref[...].astype(f32), jnp.zeros((16 - 2 - latent, channels), f32)], axis=0
    ).astype(bf16)
    listed = [nbr_ref[8 * s : 8 * s + 8, :].astype(f32) for s in range(slots // 8)]
    for half in range(2):
        row_number = (iota((atoms, atoms), 0) + half * atoms).astype(f32)
        times = jnp.zeros((atoms, atoms), f32)
        for slot in range(slots):
            times = times + jnp.where(row_number == row_of(listed[slot // 8], slot % 8, atoms), 1.0, 0.0)
        times_ref[half * atoms : (half + 1) * atoms, :] = times
    list_ref[...] = nbr_ref[...]


def charge_kernel(
    sizes,
    recv_ref,
    times_ref,
    column_ref,
    weight_ref,
    turned_ref,
    nbr_ref,
    out_ref,
    charge_ref,
):
    n_dom, n_sub = sizes
    count = out_ref.shape[0]
    atoms = nbr_ref.shape[1]
    slots = nbr_ref.shape[0]
    channels = column_ref.shape[0]
    bases = column_ref.shape[1] // atoms - 2
    latent = charge_ref.shape[0]
    ghosts = atoms // 4
    quarter = slots // 4
    dom, sub = lax.axis_index("dom"), lax.axis_index("sub")

    def device_at(dom_step, sub_step):
        return lax.rem(dom + dom_step + 2 * n_dom, n_dom) * n_sub + lax.rem(sub + sub_step + 2 * n_sub, n_sub)

    origins = tuple((-dom_step, -sub_step) for dom_step, sub_step in sends)
    data, picked = {}, {}
    for base in ((0, 0),) + origins:
        for step in ((0, 0),) + origins:
            key = (base[0] + step[0], base[1] + step[1])
            if key not in data:
                data[key] = recv_ref[device_at(*key), 0:common, :].astype(f32)
                index = row_of(data[key], 4, common).astype(i32)
                picked[key] = take_lanes(data[key], index)

    def table(key):
        return data[key], by_block([picked[(key[0] + s[0], key[1] + s[1])] for s in origins], ghosts)

    own = data[(0, 0)]
    own_table = table((0, 0))
    own_ghosts = own_table[1]

    own_lists = [nbr_ref[8 * s : 8 * s + 8, :] for s in range(slots // 8)]
    sent = [recv_ref[device_at(*key), common:, :].astype(f32) for key in origins]
    ghost_lists = []
    for r in range(4):
        for piece in range(quarter // 8):
            parts = []
            for block in range(4):
                part = sent[block][8 * piece : 8 * piece + 8]
                shift = (ghosts * (block - r)) % atoms
                parts.append(pltpu.roll(part, shift, 1) if shift else part)
            ghost_lists.append(by_block(parts, ghosts).astype(i32))

    sums = jnp.concatenate(
        [
            first_layer_sums(own_lists, [own_table], own, ghosts, bases),
            first_layer_sums(ghost_lists, [table(key) for key in origins], own_ghosts, ghosts, bases),
        ],
        axis=1,
    )
    message = dot(weight_ref[...], sums, ((1,), (0,)), highest)

    def column(number):
        return column_ref[:, number * atoms : (number + 1) * atoms]

    def turned(place):
        return turned_ref[place * channels : (place + 1) * channels, :]

    gain_first = column(bases)
    activated = normed_silu(message, jnp.concatenate([gain_first, gain_first], axis=1))
    species = jnp.concatenate([own[3:4], own_ghosts[3:4]], axis=1)
    kind_rows = iota((16, 2 * atoms), 0) - latent
    choice = jnp.where(jnp.where(species > 0.5, 1, 0) == kind_rows, 1.0, 0.0).astype(bf16)
    last = turned_ref[3 * channels : 3 * channels + 16, :]
    hidden = dot(last, choice, ((0,), (0,)))
    hidden = (hidden + dot(turned(0), activated, ((1,), (0,)))).astype(bf16)
    feats = dot(turned(1), hidden, ((1,), (0,))).astype(bf16)

    cosines, sines = cos_sin(jnp.concatenate([own, own_ghosts], axis=1))
    is_axis = iota((8, 2 * atoms), 0) < 3
    waves = jnp.concatenate([jnp.where(is_axis, cosines, 0.0), jnp.where(is_axis, sines, 0.0)], axis=0)
    chord = 1.5 - 0.5 * dot(waves, waves[:, :atoms], ((0,), (0,)), highest)
    times = times_ref[...]
    power = jnp.exp(-0.125 * chord)
    message = jnp.zeros((channels, atoms), f32)
    for basis in range(bases):
        if basis:
            power = power * power
        weighted = times * power
        high = weighted.astype(bf16)
        low = (weighted - high.astype(f32)).astype(bf16)
        mixed = dot(feats, high, ((1,), (0,))) + dot(feats, low, ((1,), (0,)))
        message = message + column(basis) * mixed
    activated = normed_silu(message, column(bases + 1))
    hidden = (hidden[:, :atoms].astype(f32) + dot(turned(2), activated, ((1,), (0,)))).astype(bf16)
    charges = dot(last, hidden, ((1,), (0,)))[:latent]
    charge_ref[...] = charges
    block = charges.astype(bf16)
    for device in range(count):
        out_ref[device] = block


def harmonic_tables(coords):
    lanes = coords.shape[1]
    step = iota((8, lanes), 0)
    big = jnp.where(step < 3, 8.0, 16.0)
    far = jnp.concatenate([coords[0:3], coords[0:3], coords[0:2]], axis=0)
    jump_cos, jump_sin = cos_sin(big * far)
    tables = []
    for axis in range(3):
        cos_low, sin_low = cos_sin(step.astype(f32) * row_of(coords, axis, 8))
        cosines, sines = [cos_low], [sin_low]
        for jump in (axis, 3 + axis):
            c, s = row_of(jump_cos, jump, 8), row_of(jump_sin, jump, 8)
            cosines.append(cos_low * c - sin_low * s)
            sines.append(sin_low * c + cos_low * s)
        tables.append((cosines, sines))
    return tables


def pair_rows(first, second):
    lanes = first[0].shape[1]
    lower = iota((8, lanes), 0) < 4

    def of(number):
        return row_of(first[number // 8], number % 8, 8)

    groups = [of(h) * second[0] for h in range(21)]
    groups += [of(h) * second[1] for h in range(19)]
    swapped = pltpu.roll(second[2], 4, 0)
    tail = jnp.where(lower, second[2], swapped)
    groups += [jnp.where(lower, of(2 * g), of(2 * g + 1)) * tail for g in range(7)]
    groups.append(of(0) * swapped)
    return groups


def pair_values(numbers):
    tail = numbers - 320
    first = jnp.where(
        numbers < 168,
        jnp.right_shift(numbers, 3),
        jnp.where(numbers < 320, jnp.right_shift(numbers - 168, 3), jnp.where(numbers < 376, jnp.right_shift(tail, 2), 0)),
    )
    second = jnp.where(
        numbers < 168,
        jnp.bitwise_and(numbers, 7),
        jnp.where(
            numbers < 320, jnp.bitwise_and(numbers, 7) + 8, jnp.where(numbers < 376, jnp.bitwise_and(tail, 3) + 16, 20)
        ),
    )
    return first, second


def fill_products(first, second, kinds, spot, grid_ref):
    for kind in kinds:
        groups = pair_rows(first[kind // 2], second[kind % 2])
        for at in range(0, pair_groups, 2):
            start = (kind * pair_groups + at) * 8
            grid_ref[start : start + 16, spot] = jnp.concatenate(groups[at : at + 2], axis=0).astype(bf16)


def fill_grid(recv_ref, device, place, grid_ref, third_ref, kinds, skipped=0, flat_ref=None):
    atoms = recv_ref.shape[2]
    tables = harmonic_tables(recv_ref[device, 0:common, :].astype(f32))
    spot = pl.ds(pl.multiple_of(place * atoms, atoms), atoms)
    later = pl.ds(pl.multiple_of((place + skipped) * atoms, atoms), atoms)
    for kind in range(2):
        for piece in range(3):
            third_ref[24 * kind + 8 * piece : 24 * kind + 8 * piece + 8, later] = tables[2][kind][piece]
    if flat_ref is not None:
        for number, table in enumerate((tables[0][1], tables[1][0], tables[1][1])):
            for piece in range(3):
                flat_ref[24 * number + 8 * piece : 24 * number + 8 * piece + 8, later] = table[piece]
    fill_products(tables[0], tables[1], kinds, spot, grid_ref)


def own_tables(recv_ref, sizes):
    device = lax.axis_index("dom") * sizes[1] + lax.axis_index("sub")
    return harmonic_tables(recv_ref[device, 0:common, :].astype(f32))


def own_side(recv_ref, sizes, right_ref):
    atoms = recv_ref.shape[2]
    tables = own_tables(recv_ref, sizes)
    first, second = pair_values(iota((pairs, atoms), 0))
    first, second = first.astype(f32), second.astype(f32)
    basis = [jnp.concatenate(pair_rows(tables[0][kind // 2], tables[1][kind % 2]), axis=0) for kind in range(4)]
    along_x = [-first * basis[2], -first * basis[3], first * basis[0], first * basis[1]]
    along_y = [-second * basis[1], second * basis[0], -second * basis[3], second * basis[2]]
    for d, part in enumerate((basis, along_x, along_y)):
        for kind in range(4):
            right_ref[kind * pairs : (kind + 1) * pairs, d * atoms : (d + 1) * atoms] = part[kind].astype(bf16)


def grid_kernel(sizes, recv_ref, wave_ref, out_ref, side_ref, third_ref, flat_ref, mask_ref, grid_ref, right_ref, sems):
    chunks, _, width = out_ref.shape
    atoms = recv_ref.shape[2]
    blocks = width // atoms
    copies = [pltpu.make_async_copy(grid_ref.at[c], out_ref.at[c], sems.at[c]) for c in range(chunks)]
    copies.append(pltpu.make_async_copy(right_ref, side_ref, sems.at[chunks]))
    own_side(recv_ref, sizes, right_ref)
    copies[chunks].start()
    for c in range(chunks):

        def one(place, carry):
            fill_grid(recv_ref, c * blocks + place, place, grid_ref.at[c], third_ref, (0, 1), c * blocks, flat_ref)
            return carry

        lax.fori_loop(0, blocks, one, 0)
        copies[c].start()
    mask_ref[...] = wave_mask(wave_ref)
    for copy in copies:
        copy.wait()


def left_rows(sum_ref, third_ref, left_ref, latent, device, spot):
    charge = sum_ref[device, 0:latent, :].astype(f32)
    left = []
    for kind in range(2):
        for m in range(harmonics):
            left.append(charge * jnp.broadcast_to(third_ref[24 * kind + m : 24 * kind + m + 1, spot], charge.shape))
    for at in range(0, 2 * harmonics, 2):
        left_ref[at * latent : (at + 2) * latent, spot] = jnp.concatenate(left[at : at + 2], axis=0).astype(bf16)


def tiled_ewald_kernel(
    total_atoms,
    sizes,
    sum_ref,
    charge_ref,
    recv_ref,
    third_ref,
    flat_ref,
    mask_ref,
    side_ref,
    grid_ref,
    pot_ref,
    force_ref,
    left_ref,
    prod_ref,
    mix_ref,
    held_ref,
    right_ref,
    sems,
):
    chunks, half, width = grid_ref.shape
    atoms = recv_ref.shape[2]
    copies = [
        pltpu.make_async_copy(grid_ref.at[c], held_ref.at[0:half, c * width : (c + 1) * width], sems.at[c])
        for c in range(chunks)
    ]
    copies.append(pltpu.make_async_copy(side_ref, right_ref, sems.at[chunks]))
    for copy in copies[:chunks]:
        copy.start()
    latent = charge_ref.shape[0]
    unroll = math.gcd(sum_ref.shape[0], 2)

    def some(step, carry):
        for part in range(unroll):
            place = step * unroll + part
            spot = pl.ds(pl.multiple_of(place * atoms, atoms), atoms)
            left_rows(sum_ref, third_ref, left_ref, latent, place, spot)
            x_sin, y_cos, y_sin = (
                [flat_ref[24 * number + 8 * piece : 24 * number + 8 * piece + 8, spot] for piece in range(3)]
                for number in range(3)
            )
            fill_products((None, x_sin), (y_cos, y_sin), (2, 3), spot, held_ref)
        return carry

    lax.fori_loop(0, sum_ref.shape[0] // unroll, some, 0)
    for copy in copies[:chunks]:
        copy.wait()
    copies[chunks].start()
    prod_ref[...] = dot(left_ref[...], held_ref[...], ((1,), (1,)))
    copies[chunks].wait()
    apply_sums(total_atoms, sizes, charge_ref, recv_ref, right_ref, pot_ref, force_ref, prod_ref, mask_ref, mix_ref)


def chunked_ewald_kernel(
    total_atoms,
    sizes,
    sum_ref,
    charge_ref,
    recv_ref,
    wave_ref,
    pot_ref,
    force_ref,
    left_ref,
    prod_ref,
    mix_ref,
    grid_ref,
    third_ref,
    right_ref,
    mask_ref,
):
    atoms = charge_ref.shape[1]
    chunk = grid_ref.shape[1] // atoms
    own_side(recv_ref, sizes, right_ref)
    prod_ref[...] = jnp.zeros(prod_ref.shape, f32)
    mask_ref[...] = wave_mask(wave_ref)

    def whole_chunk(number, carry):
        def one(place, inner):
            fill_grid(recv_ref, number * chunk + place, place, grid_ref, third_ref, range(4))
            spot = pl.ds(pl.multiple_of(place * atoms, atoms), atoms)
            left_rows(sum_ref, third_ref, left_ref, charge_ref.shape[0], number * chunk + place, spot)
            return inner

        lax.fori_loop(0, chunk, one, 0)

        def tile(column, inner):
            spot = pl.ds(pl.multiple_of(column * 256, 256), 256)
            prod_ref[:, spot] = prod_ref[:, spot] + dot(left_ref[...], grid_ref[spot, :], ((1,), (1,)))
            return inner

        return lax.fori_loop(0, 4 * pairs // 256, tile, carry)

    lax.fori_loop(0, sum_ref.shape[0] // chunk, whole_chunk, 0)
    apply_sums(total_atoms, sizes, charge_ref, recv_ref, right_ref, pot_ref, force_ref, prod_ref, mask_ref, mix_ref)


def apply_sums(total_atoms, sizes, charge_ref, recv_ref, right_ref, pot_ref, force_ref, prod_ref, mask_ref, mix_ref):
    latent, atoms = charge_ref.shape
    first, second = pair_values(iota((8, pairs), 1))
    flat = (first * first + second * second).astype(f32)
    for m in range(harmonics):
        square = flat + float(m * m)
        square = jnp.maximum(square, 1.0)
        decay = jnp.exp(-smearing * square) / square
        for block in range(lane_blocks):
            factor = decay[:, block * 128 : (block + 1) * 128]

            def cell(side, third):
                row = (block * 2 + side) * signed + third + reach - 1
                return jnp.broadcast_to(mask_ref[row : row + 1, :], (8, 128)) * factor

            up = [cell(side, m) for side in range(2)]
            if 0 < m < reach:
                down = [cell(side, -m) for side in range(2)]
                upper = [up[side] + down[side] for side in range(2)]
                lower = [up[side] - down[side] for side in range(2)]
            else:
                upper = lower = up
            weight = (upper[0] + upper[1], upper[0] - upper[1], lower[0] + lower[1], lower[0] - lower[1])

            def at(u, v, w):
                row = (u * harmonics + m) * latent
                col = (v * 2 + w) * pairs + block * 128
                return slice(row, row + latent), slice(col, col + 128)

            real = (at(0, 0, 0), at(0, 1, 1), at(1, 1, 0), at(1, 0, 1))
            imag = (at(0, 1, 0), at(0, 0, 1), at(1, 0, 0), at(1, 1, 1))
            for places, signs in ((real, (1, -1, -1, -1)), (imag, (1, 1, 1, -1))):
                values = [prod_ref[place] for place in places]
                for j, place in enumerate(places):
                    mixed = None
                    for i, value in enumerate(values):
                        term = weight[i ^ j] * value
                        if mixed is None:
                            mixed = term if signs[i] == signs[j] else -term
                        else:
                            mixed = mixed + term if signs[i] == signs[j] else mixed - term
                    mix_ref[place] = mixed

    tables = own_tables(recv_ref, sizes)
    product = dot(mix_ref[...].astype(bf16), right_ref[...], ((1,), (0,)))
    potential = jnp.zeros((latent, atoms), f32)
    slopes = [jnp.zeros((latent, atoms), f32) for _ in range(3)]
    for u in range(2):
        for m in range(harmonics):
            factor = row_of(tables[2][u][m // 8], m % 8, latent)
            turned = row_of(tables[2][1 - u][m // 8], m % 8, latent) * float(m if u else -m)
            row = (u * harmonics + m) * latent
            part = [product[row : row + latent, d * atoms : (d + 1) * atoms] for d in range(3)]
            potential = potential + factor * part[0]
            slopes[0] = slopes[0] + factor * part[1]
            slopes[1] = slopes[1] + factor * part[2]
            slopes[2] = slopes[2] + turned * part[0]
    scale = 1.0 / math.sqrt(total_atoms)
    pot_ref[...] = potential * scale
    charge = charge_ref[...]
    for d in range(3):
        force_ref[d : d + 1, :] = jnp.sum(charge * slopes[d], axis=0, keepdims=True) * -scale


def vmem(count):
    return [pl.BlockSpec(memory_space=pltpu.VMEM)] * count


def per_device(
    positions,
    species,
    neighbours,
    ghost_rows,
    wavevectors,
    embedding,
    w_in,
    radial,
    norm_gain,
    w_out,
    w_charge,
):
    axes = ("dom", "sub")
    sizes = (lax.axis_size("dom"), lax.axis_size("sub"))
    count = sizes[0] * sizes[1]
    atoms = positions.shape[1]
    latent = w_charge.shape[1]
    slots = neighbours.shape[0]
    params = pltpu.CompilerParams(vmem_limit_bytes=32 * 1024 * 1024)
    outgoing = pl.pallas_call(
        functools.partial(pack_kernel, sizes),
        out_shape=jax.ShapeDtypeStruct((count, common + slots // 4, atoms), bf16),
        in_specs=vmem(4),
        out_specs=vmem(1)[0],
    )(positions, species[None, :], neighbours, ghost_rows)
    received = lax.all_to_all(outgoing, axes, 0, 0, tiled=True)
    channels = w_in.shape[1]
    bases = radial.shape[1]
    ready = pl.pallas_call(
        ready_kernel,
        out_shape=(
            jax.ShapeDtypeStruct((2 * atoms, atoms), f32),
            jax.ShapeDtypeStruct((channels, (bases + 2) * atoms), f32),
            jax.ShapeDtypeStruct((channels, 16 * bases), f32),
            jax.ShapeDtypeStruct((3 * channels + 16, channels), bf16),
            jax.ShapeDtypeStruct((slots, atoms), i32),
        ),
        in_specs=vmem(7),
        out_specs=tuple(vmem(5)),
        compiler_params=params,
    )(neighbours, embedding, w_in, radial, norm_gain, w_out, w_charge.T)
    outgoing, charges = pl.pallas_call(
        functools.partial(charge_kernel, sizes),
        out_shape=(
            jax.ShapeDtypeStruct((count, latent, atoms), bf16),
            jax.ShapeDtypeStruct((latent, atoms), f32),
        ),
        in_specs=vmem(6),
        out_specs=tuple(vmem(2)),
        compiler_params=params,
    )(received, *ready)
    sums = lax.all_to_all(outgoing, axes, 0, 0, tiled=True)
    chunk = math.gcd(count, 32)
    rows = latent * 2 * harmonics
    results = (
        jax.ShapeDtypeStruct((latent, atoms), f32),
        jax.ShapeDtypeStruct((3, atoms), f32),
    )
    tables = (
        ((4 * pairs, chunk * atoms), bf16),
        ((48, chunk * atoms), f32),
        ((4 * pairs, 3 * atoms), bf16),
    )
    scratch = [
        pltpu.VMEM((rows, chunk * atoms), bf16),
        pltpu.VMEM((rows, 4 * pairs), f32),
        pltpu.VMEM((rows, 4 * pairs), f32),
    ]
    if chunk < count:
        return pl.pallas_call(
            functools.partial(chunked_ewald_kernel, atoms * count, sizes),
            out_shape=results,
            in_specs=vmem(4),
            out_specs=tuple(vmem(2)),
            scratch_shapes=scratch + [pltpu.VMEM(*table) for table in tables] + [pltpu.VMEM((mask_rows, 128), f32)],
        )(sums, charges, received, wavevectors)
    chunks = count // math.gcd(count, 4)
    hbm = pl.BlockSpec(memory_space=pltpu.HBM)
    grid_shape = (chunks, 2 * pairs, count * atoms // chunks)
    grid, side, third, flat, mask = pl.pallas_call(
        functools.partial(grid_kernel, sizes),
        out_shape=(
            pltpu.HBM(grid_shape, bf16),
            pltpu.HBM(*tables[2]),
            jax.ShapeDtypeStruct(*tables[1]),
            jax.ShapeDtypeStruct((72, count * atoms), f32),
            jax.ShapeDtypeStruct((mask_rows, 128), f32),
        ),
        in_specs=vmem(2),
        out_specs=(hbm, hbm, *vmem(3)),
        scratch_shapes=[
            pltpu.VMEM(grid_shape, bf16),
            pltpu.VMEM(*tables[2]),
            pltpu.SemaphoreType.DMA((chunks + 1,)),
        ],
        compiler_params=params,
    )(received, wavevectors)
    return pl.pallas_call(
        functools.partial(tiled_ewald_kernel, atoms * count, sizes),
        out_shape=results,
        in_specs=vmem(6) + [hbm, hbm],
        out_specs=tuple(vmem(2)),
        scratch_shapes=scratch
        + [pltpu.VMEM(*tables[0]), pltpu.VMEM(*tables[2]), pltpu.SemaphoreType.DMA((chunks + 1,))],
        compiler_params=params,
    )(
        sums,
        charges,
        received,
        third,
        flat,
        mask,
        pltpu.with_memory_space_constraint(side, pltpu.HBM),
        pltpu.with_memory_space_constraint(grid, pltpu.HBM),
    )


def solution(mesh):
    split = P(None, ("dom", "sub"))
    return jax.shard_map(
        per_device,
        mesh=mesh,
        in_specs=(split, P(("dom", "sub")), split, split) + (P(),) * 7,
        out_specs=(split, split),
        check_vma=False,
    )
```

```python
import functools
import math

import jax
import jax.numpy as jnp
from jax import lax
from jax.experimental import pallas as pl
from jax.experimental.pallas import tpu as pltpu
from jax.sharding import PartitionSpec as P

f32, bf16, i32 = jnp.float32, jnp.bfloat16, jnp.int32
smearing = 0.005
epsilon = 1e-05
highest = lax.Precision.HIGHEST

reach = 20
harmonics = reach + 1
signed = 2 * reach
pair_groups = 48
pairs = 8 * pair_groups
lane_blocks = pairs // 128
mask_rows = lane_blocks * 2 * signed
common = 8

sin_terms = (3.14159258, -5.16770688, 2.55003138, -0.59804517, 0.07722013)
cos_terms = (0.99999995, -4.93479286, 4.05841191, -1.33188016, 0.21969679)
sends = ((1, 0), (-1, 0), (0, 1), (0, -1))
ghost_order = (1, 0, 3, 2)


def poly(terms, square):
    total = jnp.full_like(square, terms[-1])
    for term in terms[-2::-1]:
        total = total * square + term
    return total


def sin_pi(turns):
    rest = turns - jnp.round(turns)
    return rest * poly(sin_terms, rest * rest)


def cos_sin(turns):
    rest = turns - jnp.round(turns)
    square = rest * rest
    half_sin = rest * poly(sin_terms, square)
    half_cos = poly(cos_terms, square)
    return 1.0 - 2.0 * half_sin * half_sin, 2.0 * half_sin * half_cos


def iota(shape, axis):
    return lax.broadcasted_iota(i32, shape, axis)


def lanes_of(shape, width):
    return lax.div(iota(shape, len(shape) - 1), jnp.int32(width))


def by_block(parts, width):
    which = lanes_of(parts[0].shape, width)
    out = parts[-1]
    for number in range(len(parts) - 2, -1, -1):
        out = jnp.where(which == number, parts[number], out)
    return out


def row_of(values, row, count):
    return jnp.broadcast_to(values[row : row + 1], (count,) + values.shape[1:])


def take_lanes(row_values, index):
    return jnp.take_along_axis(row_values, index, axis=1)


def dot(left, right, dims, precision=None):
    return lax.dot_general(left, right, ((dims[0], dims[1]), ((), ())), precision=precision, preferred_element_type=f32)


def pack_kernel(sizes, pos_ref, spec_ref, nbr_ref, rows_ref, out_ref):
    n_dom, n_sub = sizes
    count, _, atoms = out_ref.shape
    ghosts = rows_ref.shape[1]
    slots = nbr_ref.shape[0]
    quarter = slots // 4
    order = jnp.concatenate([rows_ref[row : row + 1, :] for row in ghost_order], axis=1)
    head = jnp.concatenate(
        [
            pos_ref[...].astype(f32),
            spec_ref[...].astype(f32),
            order.astype(f32),
            jnp.zeros((common - 5, atoms), f32),
        ],
        axis=0,
    )
    whole = jnp.concatenate([head, jnp.zeros((quarter, atoms), f32)], axis=0).astype(bf16)
    for device in range(count):
        out_ref[device] = whole
    index = jnp.broadcast_to(order, (8, atoms))
    lists = [take_lanes(nbr_ref[8 * s : 8 * s + 8, :], index).astype(f32) for s in range(slots // 8)]
    per = quarter // 8
    dom, sub = lax.axis_index("dom"), lax.axis_index("sub")
    for block, (dom_step, sub_step) in enumerate(sends):
        rows = []
        for piece in range(per):
            parts = [
                pltpu.roll(lists[r * per + piece], (ghosts * (r - block)) % atoms, 1) if r != block else lists[r * per + piece]
                for r in range(4)
            ]
            rows.append(by_block(parts, ghosts))
        target = lax.rem(dom + dom_step + n_dom, n_dom) * n_sub + lax.rem(sub + sub_step + n_sub, n_sub)
        out_ref[target, common:, :] = jnp.concatenate(rows, axis=0).astype(bf16)


def first_layer_sums(lists, tables, centre, ghosts, bases):
    total = [[None] * bases for _ in range(2)]
    for listed in lists:
        index = jnp.maximum(listed, 0)
        low = jnp.bitwise_and(index, 127)
        is_ghost = index >= 128
        found = []
        for quantity in range(4):
            parts = [
                jnp.where(is_ghost, take_lanes(row_of(outer, quantity, 8), low), take_lanes(row_of(inner, quantity, 8), low))
                for inner, outer in tables
            ]
            found.append(by_block(parts, ghosts) if len(parts) > 1 else parts[0])
        chord = jnp.zeros(low.shape, f32)
        for axis in range(3):
            wave = sin_pi(found[axis] - row_of(centre, axis, 8))
            chord = chord + wave * wave
        first = jnp.where(listed >= 0, jnp.exp(-0.125 * chord), 0.0)
        for kind in range(2):
            power = jnp.where((found[3] > 0.5) if kind else (found[3] <= 0.5), first, 0.0)
            for basis in range(bases):
                if basis:
                    power = power * power
                total[kind][basis] = power if total[kind][basis] is None else total[kind][basis] + power
    return jnp.concatenate(total[0] + total[1], axis=0)


def wave_mask(wave_ref):
    first = wave_ref[0:1, :]
    second = wave_ref[1:2, :]
    third = wave_ref[2:3, :]
    size = jnp.abs(second)
    pair = jnp.where(
        size < 8,
        8 * first + size,
        jnp.where(size < 16, 160 + 8 * first + size, jnp.where(size < 20, 304 + 4 * first + size, 376)),
    )
    side = jnp.where(second < 0, 1, 0)
    row = (jnp.right_shift(pair, 7) * 2 + side) * signed + third + (reach - 1)
    lane = jnp.bitwise_and(pair, 127)
    total_k = row.shape[1]
    left = jnp.where(iota((mask_rows, total_k), 0) == row, 1.0, 0.0).astype(bf16)
    right = jnp.where(iota((128, total_k), 0) == lane, 1.0, 0.0).astype(bf16)
    return dot(left, right, ((1,), (1,)))


def normed_silu(message, gain):
    normed = message * lax.rsqrt(jnp.mean(message * message, axis=0, keepdims=True) + epsilon) * gain
    return (normed / (1.0 + jnp.exp(-normed))).astype(bf16)


def ready_kernel(nbr_ref, emb_ref, w_in_ref, radial_ref, gain_ref, w_out_ref, w_charge_ref, times_ref, column_ref, weight_ref, turned_ref, list_ref):
    atoms = nbr_ref.shape[1]
    slots = nbr_ref.shape[0]
    bases = radial_ref.shape[1]
    channels = w_in_ref.shape[1]
    latent = w_charge_ref.shape[0]

    kinds = jnp.concatenate([emb_ref[...].astype(f32), jnp.zeros((6, channels), f32)], axis=0).astype(bf16)
    two_feats = dot(kinds, w_in_ref[0], ((1,), (0,))).astype(bf16).astype(f32)
    radial_first = radial_ref[0].astype(f32)
    weights = jnp.concatenate(
        [
            jnp.broadcast_to(radial_first[basis : basis + 1] * two_feats[kind : kind + 1], (8, channels))
            for kind in range(2)
            for basis in range(bases)
        ],
        axis=0,
    )
    weight_ref[...] = weights.T
    params = jnp.concatenate(
        [radial_ref[1].astype(f32), gain_ref[...].astype(f32), jnp.zeros((16 - bases - 2, channels), f32)], axis=0
    ).astype(bf16)
    width = column_ref.shape[1]
    spread = jnp.where(iota((16, width), 0) == lanes_of((16, width), atoms), 1.0, 0.0).astype(bf16)
    column_ref[...] = dot(params, spread, ((0,), (0,)))
    for place, weight in enumerate((w_out_ref[0], w_in_ref[1], w_out_ref[1])):
        turned_ref[place * channels : (place + 1) * channels, :] = weight.astype(f32).T.astype(bf16)
    turned_ref[3 * channels : 3 * channels + 16, :] = jnp.concatenate(
        [w_charge_ref[...].astype(f32), emb_ref[...].astype(f32), jnp.zeros((16 - 2 - latent, channels), f32)], axis=0
    ).astype(bf16)
    listed = [nbr_ref[8 * s : 8 * s + 8, :].astype(f32) for s in range(slots // 8)]
    for half in range(2):
        row_number = (iota((atoms, atoms), 0) + half * atoms).astype(f32)
        times = jnp.zeros((atoms, atoms), f32)
        for slot in range(slots):
            times = times + jnp.where(row_number == row_of(listed[slot // 8], slot % 8, atoms), 1.0, 0.0)
        times_ref[half * atoms : (half + 1) * atoms, :] = times
    list_ref[...] = nbr_ref[...]


def charge_kernel(
    sizes,
    recv_ref,
    times_ref,
    column_ref,
    weight_ref,
    turned_ref,
    nbr_ref,
    out_ref,
    charge_ref,
):
    n_dom, n_sub = sizes
    count = out_ref.shape[0]
    atoms = nbr_ref.shape[1]
    slots = nbr_ref.shape[0]
    channels = column_ref.shape[0]
    bases = column_ref.shape[1] // atoms - 2
    latent = charge_ref.shape[0]
    ghosts = atoms // 4
    quarter = slots // 4
    dom, sub = lax.axis_index("dom"), lax.axis_index("sub")

    def device_at(dom_step, sub_step):
        return lax.rem(dom + dom_step + 2 * n_dom, n_dom) * n_sub + lax.rem(sub + sub_step + 2 * n_sub, n_sub)

    origins = tuple((-dom_step, -sub_step) for dom_step, sub_step in sends)
    data, picked = {}, {}
    for base in ((0, 0),) + origins:
        for step in ((0, 0),) + origins:
            key = (base[0] + step[0], base[1] + step[1])
            if key not in data:
                data[key] = recv_ref[device_at(*key), 0:common, :].astype(f32)
                index = row_of(data[key], 4, common).astype(i32)
                picked[key] = take_lanes(data[key], index)

    def table(key):
        return data[key], by_block([picked[(key[0] + s[0], key[1] + s[1])] for s in origins], ghosts)

    own = data[(0, 0)]
    own_table = table((0, 0))
    own_ghosts = own_table[1]

    own_lists = [nbr_ref[8 * s : 8 * s + 8, :] for s in range(slots // 8)]
    sent = [recv_ref[device_at(*key), common:, :].astype(f32) for key in origins]
    ghost_lists = []
    for r in range(4):
        for piece in range(quarter // 8):
            parts = []
            for block in range(4):
                part = sent[block][8 * piece : 8 * piece + 8]
                shift = (ghosts * (block - r)) % atoms
                parts.append(pltpu.roll(part, shift, 1) if shift else part)
            ghost_lists.append(by_block(parts, ghosts).astype(i32))

    sums = jnp.concatenate(
        [
            first_layer_sums(own_lists, [own_table], own, ghosts, bases),
            first_layer_sums(ghost_lists, [table(key) for key in origins], own_ghosts, ghosts, bases),
        ],
        axis=1,
    )
    message = dot(weight_ref[...], sums, ((1,), (0,)), highest)

    def column(number):
        return column_ref[:, number * atoms : (number + 1) * atoms]

    def turned(place):
        return turned_ref[place * channels : (place + 1) * channels, :]

    gain_first = column(bases)
    activated = normed_silu(message, jnp.concatenate([gain_first, gain_first], axis=1))
    species = jnp.concatenate([own[3:4], own_ghosts[3:4]], axis=1)
    kind_rows = iota((16, 2 * atoms), 0) - latent
    choice = jnp.where(jnp.where(species > 0.5, 1, 0) == kind_rows, 1.0, 0.0).astype(bf16)
    last = turned_ref[3 * channels : 3 * channels + 16, :]
    hidden = dot(last, choice, ((0,), (0,)))
    hidden = (hidden + dot(turned(0), activated, ((1,), (0,)))).astype(bf16)
    feats = dot(turned(1), hidden, ((1,), (0,))).astype(bf16)

    cosines, sines = cos_sin(jnp.concatenate([own, own_ghosts], axis=1))
    is_axis = iota((8, 2 * atoms), 0) < 3
    waves = jnp.concatenate([jnp.where(is_axis, cosines, 0.0), jnp.where(is_axis, sines, 0.0)], axis=0)
    chord = 1.5 - 0.5 * dot(waves, waves[:, :atoms], ((0,), (0,)), highest)
    times = times_ref[...]
    power = jnp.exp(-0.125 * chord)
    message = jnp.zeros((channels, atoms), f32)
    for basis in range(bases):
        if basis:
            power = power * power
        weighted = times * power
        high = weighted.astype(bf16)
        low = (weighted - high.astype(f32)).astype(bf16)
        mixed = dot(feats, high, ((1,), (0,))) + dot(feats, low, ((1,), (0,)))
        message = message + column(basis) * mixed
    activated = normed_silu(message, column(bases + 1))
    hidden = (hidden[:, :atoms].astype(f32) + dot(turned(2), activated, ((1,), (0,)))).astype(bf16)
    charges = dot(last, hidden, ((1,), (0,)))[:latent]
    charge_ref[...] = charges
    block = charges.astype(bf16)
    for device in range(count):
        out_ref[device] = block


def harmonic_tables(coords):
    lanes = coords.shape[1]
    step = iota((8, lanes), 0)
    big = jnp.where(step < 3, 8.0, 16.0)
    far = jnp.concatenate([coords[0:3], coords[0:3], coords[0:2]], axis=0)
    jump_cos, jump_sin = cos_sin(big * far)
    tables = []
    for axis in range(3):
        cos_low, sin_low = cos_sin(step.astype(f32) * row_of(coords, axis, 8))
        cosines, sines = [cos_low], [sin_low]
        for jump in (axis, 3 + axis):
            c, s = row_of(jump_cos, jump, 8), row_of(jump_sin, jump, 8)
            cosines.append(cos_low * c - sin_low * s)
            sines.append(sin_low * c + cos_low * s)
        tables.append((cosines, sines))
    return tables


def pair_rows(first, second):
    lanes = first[0].shape[1]
    lower = iota((8, lanes), 0) < 4

    def of(number):
        return row_of(first[number // 8], number % 8, 8)

    groups = [of(h) * second[0] for h in range(21)]
    groups += [of(h) * second[1] for h in range(19)]
    swapped = pltpu.roll(second[2], 4, 0)
    tail = jnp.where(lower, second[2], swapped)
    groups += [jnp.where(lower, of(2 * g), of(2 * g + 1)) * tail for g in range(7)]
    groups.append(of(0) * swapped)
    return groups


def pair_values(numbers):
    tail = numbers - 320
    first = jnp.where(
        numbers < 168,
        jnp.right_shift(numbers, 3),
        jnp.where(numbers < 320, jnp.right_shift(numbers - 168, 3), jnp.where(numbers < 376, jnp.right_shift(tail, 2), 0)),
    )
    second = jnp.where(
        numbers < 168,
        jnp.bitwise_and(numbers, 7),
        jnp.where(
            numbers < 320, jnp.bitwise_and(numbers, 7) + 8, jnp.where(numbers < 376, jnp.bitwise_and(tail, 3) + 16, 20)
        ),
    )
    return first, second


def fill_products(first, second, kinds, spot, grid_ref):
    for kind in kinds:
        groups = pair_rows(first[kind // 2], second[kind % 2])
        for at in range(0, pair_groups, 2):
            start = (kind * pair_groups + at) * 8
            grid_ref[start : start + 16, spot] = jnp.concatenate(groups[at : at + 2], axis=0).astype(bf16)


def fill_grid(recv_ref, device, place, grid_ref, third_ref, kinds, skipped=0, flat_ref=None):
    atoms = recv_ref.shape[2]
    tables = harmonic_tables(recv_ref[device, 0:common, :].astype(f32))
    spot = pl.ds(pl.multiple_of(place * atoms, atoms), atoms)
    later = pl.ds(pl.multiple_of((place + skipped) * atoms, atoms), atoms)
    for kind in range(2):
        for piece in range(3):
            third_ref[24 * kind + 8 * piece : 24 * kind + 8 * piece + 8, later] = tables[2][kind][piece]
    if flat_ref is not None:
        for number, table in enumerate((tables[0][1], tables[1][0], tables[1][1])):
            for piece in range(3):
                flat_ref[24 * number + 8 * piece : 24 * number + 8 * piece + 8, later] = table[piece]
    fill_products(tables[0], tables[1], kinds, spot, grid_ref)


def own_tables(recv_ref, sizes):
    device = lax.axis_index("dom") * sizes[1] + lax.axis_index("sub")
    return harmonic_tables(recv_ref[device, 0:common, :].astype(f32))


def own_side(recv_ref, sizes, right_ref):
    atoms = recv_ref.shape[2]
    tables = own_tables(recv_ref, sizes)
    first, second = pair_values(iota((pairs, atoms), 0))
    first, second = first.astype(f32), second.astype(f32)
    basis = [jnp.concatenate(pair_rows(tables[0][kind // 2], tables[1][kind % 2]), axis=0) for kind in range(4)]
    along_x = [-first * basis[2], -first * basis[3], first * basis[0], first * basis[1]]
    along_y = [-second * basis[1], second * basis[0], -second * basis[3], second * basis[2]]
    for d, part in enumerate((basis, along_x, along_y)):
        for kind in range(4):
            right_ref[kind * pairs : (kind + 1) * pairs, d * atoms : (d + 1) * atoms] = part[kind].astype(bf16)


def grid_kernel(sizes, recv_ref, wave_ref, out_ref, side_ref, third_ref, flat_ref, mask_ref, grid_ref, right_ref, sems):
    chunks, _, width = out_ref.shape
    atoms = recv_ref.shape[2]
    blocks = width // atoms
    copies = [pltpu.make_async_copy(grid_ref.at[c], out_ref.at[c], sems.at[c]) for c in range(chunks)]
    copies.append(pltpu.make_async_copy(right_ref, side_ref, sems.at[chunks]))
    own_side(recv_ref, sizes, right_ref)
    copies[chunks].start()
    for c in range(chunks):

        def one(place, carry):
            fill_grid(recv_ref, c * blocks + place, place, grid_ref.at[c], third_ref, (0, 1), c * blocks, flat_ref)
            return carry

        lax.fori_loop(0, blocks, one, 0)
        copies[c].start()
    mask_ref[...] = wave_mask(wave_ref)
    for copy in copies:
        copy.wait()


def left_rows(sum_ref, third_ref, left_ref, latent, device, spot):
    charge = sum_ref[device, 0:latent, :].astype(f32)
    left = []
    for kind in range(2):
        for m in range(harmonics):
            left.append(charge * jnp.broadcast_to(third_ref[24 * kind + m : 24 * kind + m + 1, spot], charge.shape))
    for at in range(0, 2 * harmonics, 2):
        left_ref[at * latent : (at + 2) * latent, spot] = jnp.concatenate(left[at : at + 2], axis=0).astype(bf16)


def tiled_ewald_kernel(
    total_atoms,
    sizes,
    sum_ref,
    charge_ref,
    recv_ref,
    third_ref,
    flat_ref,
    mask_ref,
    side_ref,
    grid_ref,
    pot_ref,
    force_ref,
    left_ref,
    prod_ref,
    mix_ref,
    held_ref,
    right_ref,
    sems,
):
    chunks, half, width = grid_ref.shape
    atoms = recv_ref.shape[2]
    copies = [
        pltpu.make_async_copy(grid_ref.at[c], held_ref.at[0:half, c * width : (c + 1) * width], sems.at[c])
        for c in range(chunks)
    ]
    copies.append(pltpu.make_async_copy(side_ref, right_ref, sems.at[chunks]))
    for copy in copies[:chunks]:
        copy.start()
    latent = charge_ref.shape[0]
    unroll = math.gcd(sum_ref.shape[0], 2)

    def some(step, carry):
        for part in range(unroll):
            place = step * unroll + part
            spot = pl.ds(pl.multiple_of(place * atoms, atoms), atoms)
            left_rows(sum_ref, third_ref, left_ref, latent, place, spot)
            x_sin, y_cos, y_sin = (
                [flat_ref[24 * number + 8 * piece : 24 * number + 8 * piece + 8, spot] for piece in range(3)]
                for number in range(3)
            )
            fill_products((None, x_sin), (y_cos, y_sin), (2, 3), spot, held_ref)
        return carry

    lax.fori_loop(0, sum_ref.shape[0] // unroll, some, 0)
    for copy in copies[:chunks]:
        copy.wait()
    copies[chunks].start()
    prod_ref[...] = dot(left_ref[...], held_ref[...], ((1,), (1,)))
    copies[chunks].wait()
    apply_sums(total_atoms, sizes, charge_ref, recv_ref, right_ref, pot_ref, force_ref, prod_ref, mask_ref, mix_ref)


def chunked_ewald_kernel(
    total_atoms,
    sizes,
    sum_ref,
    charge_ref,
    recv_ref,
    wave_ref,
    pot_ref,
    force_ref,
    left_ref,
    prod_ref,
    mix_ref,
    grid_ref,
    third_ref,
    right_ref,
    mask_ref,
):
    atoms = charge_ref.shape[1]
    chunk = grid_ref.shape[1] // atoms
    own_side(recv_ref, sizes, right_ref)
    prod_ref[...] = jnp.zeros(prod_ref.shape, f32)
    mask_ref[...] = wave_mask(wave_ref)

    def whole_chunk(number, carry):
        def one(place, inner):
            fill_grid(recv_ref, number * chunk + place, place, grid_ref, third_ref, range(4))
            spot = pl.ds(pl.multiple_of(place * atoms, atoms), atoms)
            left_rows(sum_ref, third_ref, left_ref, charge_ref.shape[0], number * chunk + place, spot)
            return inner

        lax.fori_loop(0, chunk, one, 0)

        def tile(column, inner):
            spot = pl.ds(pl.multiple_of(column * 256, 256), 256)
            prod_ref[:, spot] = prod_ref[:, spot] + dot(left_ref[...], grid_ref[spot, :], ((1,), (1,)))
            return inner

        return lax.fori_loop(0, 4 * pairs // 256, tile, carry)

    lax.fori_loop(0, sum_ref.shape[0] // chunk, whole_chunk, 0)
    apply_sums(total_atoms, sizes, charge_ref, recv_ref, right_ref, pot_ref, force_ref, prod_ref, mask_ref, mix_ref)


def apply_sums(total_atoms, sizes, charge_ref, recv_ref, right_ref, pot_ref, force_ref, prod_ref, mask_ref, mix_ref):
    latent, atoms = charge_ref.shape
    first, second = pair_values(iota((8, pairs), 1))
    flat = (first * first + second * second).astype(f32)
    for m in range(harmonics):
        square = flat + float(m * m)
        square = jnp.maximum(square, 1.0)
        decay = jnp.exp(-smearing * square) / square
        for block in range(lane_blocks):
            factor = decay[:, block * 128 : (block + 1) * 128]

            def cell(side, third):
                row = (block * 2 + side) * signed + third + reach - 1
                return jnp.broadcast_to(mask_ref[row : row + 1, :], (8, 128)) * factor

            up = [cell(side, m) for side in range(2)]
            if 0 < m < reach:
                down = [cell(side, -m) for side in range(2)]
                upper = [up[side] + down[side] for side in range(2)]
                lower = [up[side] - down[side] for side in range(2)]
            else:
                upper = lower = up
            weight = (upper[0] + upper[1], upper[0] - upper[1], lower[0] + lower[1], lower[0] - lower[1])

            def at(u, v, w):
                row = (u * harmonics + m) * latent
                col = (v * 2 + w) * pairs + block * 128
                return slice(row, row + latent), slice(col, col + 128)

            real = (at(0, 0, 0), at(0, 1, 1), at(1, 1, 0), at(1, 0, 1))
            imag = (at(0, 1, 0), at(0, 0, 1), at(1, 0, 0), at(1, 1, 1))
            for places, signs in ((real, (1, -1, -1, -1)), (imag, (1, 1, 1, -1))):
                values = [prod_ref[place] for place in places]
                for j, place in enumerate(places):
                    mixed = None
                    for i, value in enumerate(values):
                        term = weight[i ^ j] * value
                        if mixed is None:
                            mixed = term if signs[i] == signs[j] else -term
                        else:
                            mixed = mixed + term if signs[i] == signs[j] else mixed - term
                    mix_ref[place] = mixed

    tables = own_tables(recv_ref, sizes)
    product = dot(mix_ref[...].astype(bf16), right_ref[...], ((1,), (0,)))
    potential = jnp.zeros((latent, atoms), f32)
    slopes = [jnp.zeros((latent, atoms), f32) for _ in range(3)]
    for u in range(2):
        for m in range(harmonics):
            factor = row_of(tables[2][u][m // 8], m % 8, latent)
            turned = row_of(tables[2][1 - u][m // 8], m % 8, latent) * float(m if u else -m)
            row = (u * harmonics + m) * latent
            part = [product[row : row + latent, d * atoms : (d + 1) * atoms] for d in range(3)]
            potential = potential + factor * part[0]
            slopes[0] = slopes[0] + factor * part[1]
            slopes[1] = slopes[1] + factor * part[2]
            slopes[2] = slopes[2] + turned * part[0]
    scale = 1.0 / math.sqrt(total_atoms)
    pot_ref[...] = potential * scale
    charge = charge_ref[...]
    for d in range(3):
        force_ref[d : d + 1, :] = jnp.sum(charge * slopes[d], axis=0, keepdims=True) * -scale


def vmem(count):
    return [pl.BlockSpec(memory_space=pltpu.VMEM)] * count


def per_device(
    positions,
    species,
    neighbours,
    ghost_rows,
    wavevectors,
    embedding,
    w_in,
    radial,
    norm_gain,
    w_out,
    w_charge,
):
    axes = ("dom", "sub")
    sizes = (lax.axis_size("dom"), lax.axis_size("sub"))
    count = sizes[0] * sizes[1]
    atoms = positions.shape[1]
    latent = w_charge.shape[1]
    slots = neighbours.shape[0]
    params = pltpu.CompilerParams(vmem_limit_bytes=32 * 1024 * 1024)
    outgoing = pl.pallas_call(
        functools.partial(pack_kernel, sizes),
        out_shape=jax.ShapeDtypeStruct((count, common + slots // 4, atoms), bf16),
        in_specs=vmem(4),
        out_specs=vmem(1)[0],
    )(positions, species[None, :], neighbours, ghost_rows)
    received = lax.all_to_all(outgoing, axes, 0, 0, tiled=True)
    channels = w_in.shape[1]
    bases = radial.shape[1]
    ready = pl.pallas_call(
        ready_kernel,
        out_shape=(
            jax.ShapeDtypeStruct((2 * atoms, atoms), f32),
            jax.ShapeDtypeStruct((channels, (bases + 2) * atoms), f32),
            jax.ShapeDtypeStruct((channels, 16 * bases), f32),
            jax.ShapeDtypeStruct((3 * channels + 16, channels), bf16),
            jax.ShapeDtypeStruct((slots, atoms), i32),
        ),
        in_specs=vmem(7),
        out_specs=tuple(vmem(5)),
        compiler_params=params,
    )(neighbours, embedding, w_in, radial, norm_gain, w_out, w_charge.T)
    outgoing, charges = pl.pallas_call(
        functools.partial(charge_kernel, sizes),
        out_shape=(
            jax.ShapeDtypeStruct((count, latent, atoms), bf16),
            jax.ShapeDtypeStruct((latent, atoms), f32),
        ),
        in_specs=vmem(6),
        out_specs=tuple(vmem(2)),
        compiler_params=params,
    )(received, *ready)
    sums = lax.all_to_all(outgoing, axes, 0, 0, tiled=True)
    chunk = math.gcd(count, 32)
    rows = latent * 2 * harmonics
    results = (
        jax.ShapeDtypeStruct((latent, atoms), f32),
        jax.ShapeDtypeStruct((3, atoms), f32),
    )
    tables = (
        ((4 * pairs, chunk * atoms), bf16),
        ((48, chunk * atoms), f32),
        ((4 * pairs, 3 * atoms), bf16),
    )
    scratch = [
        pltpu.VMEM((rows, chunk * atoms), bf16),
        pltpu.VMEM((rows, 4 * pairs), f32),
        pltpu.VMEM((rows, 4 * pairs), f32),
    ]
    if chunk < count:
        return pl.pallas_call(
            functools.partial(chunked_ewald_kernel, atoms * count, sizes),
            out_shape=results,
            in_specs=vmem(4),
            out_specs=tuple(vmem(2)),
            scratch_shapes=scratch + [pltpu.VMEM(*table) for table in tables] + [pltpu.VMEM((mask_rows, 128), f32)],
        )(sums, charges, received, wavevectors)
    chunks = count // math.gcd(count, 8)
    hbm = pl.BlockSpec(memory_space=pltpu.HBM)
    grid_shape = (chunks, 2 * pairs, count * atoms // chunks)
    grid, side, third, flat, mask = pl.pallas_call(
        functools.partial(grid_kernel, sizes),
        out_shape=(
            pltpu.HBM(grid_shape, bf16),
            pltpu.HBM(*tables[2]),
            jax.ShapeDtypeStruct(*tables[1]),
            jax.ShapeDtypeStruct((72, count * atoms), f32),
            jax.ShapeDtypeStruct((mask_rows, 128), f32),
        ),
        in_specs=vmem(2),
        out_specs=(hbm, hbm, *vmem(3)),
        scratch_shapes=[
            pltpu.VMEM(grid_shape, bf16),
            pltpu.VMEM(*tables[2]),
            pltpu.SemaphoreType.DMA((chunks + 1,)),
        ],
        compiler_params=params,
    )(received, wavevectors)
    return pl.pallas_call(
        functools.partial(tiled_ewald_kernel, atoms * count, sizes),
        out_shape=results,
        in_specs=vmem(6) + [hbm, hbm],
        out_specs=tuple(vmem(2)),
        scratch_shapes=scratch
        + [pltpu.VMEM(*tables[0]), pltpu.VMEM(*tables[2]), pltpu.SemaphoreType.DMA((chunks + 1,))],
        compiler_params=params,
    )(
        sums,
        charges,
        received,
        third,
        flat,
        mask,
        pltpu.with_memory_space_constraint(side, pltpu.HBM),
        pltpu.with_memory_space_constraint(grid, pltpu.HBM),
    )


def solution(mesh):
    split = P(None, ("dom", "sub"))
    return jax.shard_map(
        per_device,
        mesh=mesh,
        in_specs=(split, P(("dom", "sub")), split, split) + (P(),) * 7,
        out_specs=(split, split),
        check_vma=False,
    )
```
